128 devices in a mesh: lon: 16 (over x_lo, y, core), lat: 8 (over x_hi, z).
Axes of the slice: x: 4 (x_hi: 2, x_lo: 2; x = x_hi * 2 + x_lo), y: 4, z: 4, core: 2. Of those that a mesh axis runs over, the one named last changes fastest.
Arguments:
- grad_field: float32 [32, 64, 137, 128], P('lat', 'lon'), may hold values from -6 to 6
- lat_weights: float32 [8, 3], replicated, may hold values from 0.2 to 1
- block_offsets: int32 [8, 5], replicated, may hold values from -3 to 3, as said below
- filters: bfloat16 [8, 5, 128, 128], replicated, may hold values from -0.25 to 0.25
- vertical: bfloat16 [8, 137, 137], replicated, may hold values from -0.5 to 0.5
- slot_of_band: int32 [8], replicated, may hold values from 0 to 7, each once
Outputs:
- band_control: bfloat16 [8, 32, 64, 137, 128], P('lat', 'lon')
The draws below stay inside these ranges and needn't reach their ends.
Inputs may be any that keep to these rules, and one draw needn't show every extreme that they name: `block_offsets`: each band names 5 different offsets; offset -3 is named by some band and offset 3 by some band.
All inputs are finite; a program needn't handle non-finite values.
Results may differ from the reference program's by a relative error of at most 0.0058.
Values may be sent and summed in bfloat16 or wider, within the bound.
A program may use at most 128 MiB of HBM per device.

```python
import jax
import jax.numpy as jnp
from jax import lax

LEV = 137
BLOCK = 128
NB = 8
KB = 5
REACH = 3
NLAT = 32
NLON = 8192


def draw_block_offsets(key, part):
    choices_count = 2 * REACH + 1

    def one_row(row_key):
        return jax.random.permutation(row_key, choices_count).astype(jnp.int32)
    scores = jax.vmap(one_row)(jax.random.split(jax.random.fold_in(key, 17), NB))
    scores = scores.at[0, 0].add(100).at[1, choices_count - 1].add(100)
    picked = lax.top_k(scores, KB)[1]
    return (picked - REACH).astype(jnp.int32)


def levels(stream_key, shape, pieces, smallest, largest):
    factor_of = 1.0
    for dim, blocks in pieces:
        steps = jax.random.uniform(jax.random.fold_in(jax.random.fold_in(stream_key, 6), dim), (blocks,), jnp.float32, smallest / len(pieces), largest / len(pieces))
        factor_of = factor_of * jnp.repeat(jnp.exp(steps), shape[dim] // blocks).reshape((-1,) + (1,) * (len(shape) - 1 - dim))
    return factor_of


def gaussian(key, dims, deviation, reach, cuts=(), held_as=jnp.bfloat16):
    factor_of = levels(key, dims, cuts, -0.22, 0.18) if cuts else 1.0
    entries = jax.random.normal(key, dims, jnp.float32) * deviation * factor_of
    return jnp.minimum(jnp.maximum(entries, -reach), reach).astype(held_as)


def setup_inputs(seed: int = 0) -> dict:
    arg_keys = jax.random.split(jax.random.key(seed), 7)
    return {
        "grad_field": gaussian(arg_keys[0], (NLAT, NLON // BLOCK, LEV, BLOCK), 1.0, 6.0, ((0, 8), (1, 16)), jnp.float32),
        "lat_weights": jnp.clip(jax.random.uniform(arg_keys[1], (NB, 3), jnp.float32, 0.2, 1.0), 0.2, 1.0),
        "block_offsets": draw_block_offsets(jax.random.fold_in(arg_keys[6], 71), 0),
        "filters": gaussian(arg_keys[3], (NB, KB, BLOCK, BLOCK), (BLOCK * KB) ** -0.5, 0.25),
        "vertical": gaussian(arg_keys[4], (NB, LEV, LEV), LEV ** -0.5, 0.5),
        "slot_of_band": jax.random.permutation(arg_keys[5], NB).astype(jnp.int32),
    }


def reference(grad_field, lat_weights, block_offsets, filters, vertical, slot_of_band):
    padded = jnp.pad(grad_field, ((1, 1), (0, 0), (0, 0), (0, 0)))

    def one_band(items):
        weights, offsets, filter_set, vertical_b = items
        blended = (weights[0] * padded[:-2] + weights[1] * padded[1:-1] + weights[2] * padded[2:]).astype(jnp.bfloat16)
        shape_all = blended.shape
        running = jnp.zeros((shape_all[0] * shape_all[1] * shape_all[2], shape_all[3]), jnp.float32)
        for position in range(KB):
            moved = jnp.roll(blended, -offsets[position], axis=1)
            running = running + jnp.dot(moved.reshape(-1, shape_all[3]), filter_set[position], preferred_element_type=jnp.float32)
        smoothed = running.astype(jnp.bfloat16).reshape(shape_all)
        result = jnp.einsum("ml,rqlc->rqmc", vertical_b.astype(jnp.float32), smoothed.astype(jnp.float32))
        return result.astype(jnp.bfloat16)

    results = lax.map(one_band, (lat_weights, block_offsets, filters, vertical))
    return jnp.zeros_like(results).at[slot_of_band].set(results)
```

```python
import functools

import jax
import jax.numpy as jnp
from jax import lax
from jax.experimental import pallas as pl
from jax.experimental.pallas import tpu as pltpu
from jax.sharding import PartitionSpec as P

MESH = pl.DeviceIdType.MESH
SPLIT = 1
LATE = 0


def gather_kernel(levels, pad, x_ref, f_ref, staged, blank, send_sems, first_sems, recv_sems, halo_send, halo_recv, fill_sem):
    o, t = lax.axis_index("lon"), lax.axis_index("lat")
    xh, z = t // 4, t % 4
    zp, zm = xh * 4 + (z + 1) % 4, xh * 4 + (z + 3) % 4
    xp = (1 - xh) * 4 + z
    owner_lat, core = o // 2, o % 2
    nq = 4 // SPLIT
    per = 2 * SPLIT

    barrier = pltpu.get_barrier_semaphore()

    def greet(lon, lat):
        pl.semaphore_signal(barrier, inc=1, device_id={"lon": lon, "lat": lat}, device_id_type=MESH)

    for k in range(2):
        greet(2 * t + k, owner_lat)
    for lat in (zp, zm, xp):
        greet(o, lat)

    @pl.when(o > 0)
    def _():
        greet(o - 1, t)

    @pl.when(o < 15)
    def _():
        greet(o + 1, t)

    def stage(k):
        for i in (2 * k, 2 * k + 1):
            for q in range(4):
                value = x_ref[pl.ds(i * levels * 4 + q, levels, stride=4), :]
                staged[i, q, 0:levels, :] = value.astype(jnp.bfloat16)
                staged[i, q, levels:pad, :] = jnp.zeros((pad - levels, 128), jnp.bfloat16)

    stage(0)
    edge = (o == 0).astype(jnp.int32) + (o == 15).astype(jnp.int32)
    pl.semaphore_wait(barrier, 7 - edge)

    def first(k, s):
        src = staged.at[pl.ds(2 * k, 2), pl.ds(s * nq, nq)]
        dst = f_ref.at[pl.ds(1, 2), pl.ds(4 * o + s * nq, nq)]
        far = pltpu.make_async_remote_copy(
            src, dst, first_sems.at[k, s], recv_sems.at[0, 0, core * SPLIT + s],
            device_id={"lon": 2 * t + k, "lat": owner_lat}, device_id_type=MESH,
        )
        near = pltpu.make_async_copy(src, dst, recv_sems.at[0, 0, core * SPLIT + s])
        mine = (owner_lat == t) & (core == k)
        return far, near, mine

    def start_first(k):
        for s in range(SPLIT):
            far, near, mine = first(k, s)

            @pl.when(mine)
            def _():
                near.start()

            @pl.when(jnp.logical_not(mine))
            def _():
                far.start()

    start_first(0)
    stage(1)
    start_first(1)

    @pl.when(edge > 0)
    def _():
        blank[...] = jnp.zeros_like(blank)
        row = jnp.where(o == 0, 0, 3)
        fills = [pltpu.make_async_copy(blank, f_ref.at[row, pl.ds(c * 8, 8)], fill_sem.at[c]) for c in range(8)]
        for f in fills:
            f.start()
        for f in fills:
            f.wait()

    sends = []

    def rows_of(dx, dz, j):
        owner = ((xh + dx) % 2) * 4 + (z + dz) % 4
        return pl.ds(owner * 8 + j * nq, nq)

    def piece(dx, dz, j):
        return f_ref.at[pl.ds(1, 2), rows_of(dx, dz, j)]

    def send(dx, dz, j, to, there):
        ref = piece(dx, dz, j)
        copy = pltpu.make_async_remote_copy(
            ref, ref, send_sems.at[len(sends)], recv_sems.at[there[0], there[1], j],
            device_id={"lon": o, "lat": to}, device_id_type=MESH,
        )
        copy.start()
        sends.append(copy)

    def halo(dx, dz, j, side):
        q = rows_of(dx, dz, j)
        src = f_ref.at[1 + side, q]
        dst = f_ref.at[3 - 3 * side, q]
        slot = (dx * 4 + dz) * per + j
        return pltpu.make_async_remote_copy(
            src, dst, halo_send.at[side, slot], halo_recv.at[side, slot],
            device_id={"lon": o - 1 + 2 * side, "lat": t}, device_id_type=MESH,
        )

    def each_halo(action):
        @pl.when(o > 0)
        def _():
            action(0)

        @pl.when(o < 15)
        def _():
            action(1)

    def arrive(dx, dz, j):
        ref = piece(dx, dz, j)
        pltpu.make_async_copy(ref, ref, recv_sems.at[dx, dz, j]).wait()
        late = j >= per - LATE
        ring = dx == 0 or not late
        if dx == 0 and (dz == 0 or late):
            if dz == 0:
                send(dx, dz, j, xp, (1, 0))
        if ring and dz == 0:
            send(dx, dz, j, zp, (dx, 3))
            send(dx, dz, j, zm, (dx, 1))
        if ring and dz == 3 and j < per // 2:
            send(dx, dz, j, zp, (dx, 2))
        if ring and dz == 1 and j >= per // 2:
            send(dx, dz, j, zm, (dx, 2))
        if dx == 0 and dz != 0 and late:
            send(dx, dz, j, xp, (1, dz))
        each_halo(lambda side: halo(dx, dz, j, side).start())

    order = [(0, 0), (0, 1), (0, 3), (1, 0), (0, 2), (1, 1), (1, 3), (1, 2)]
    for dx, dz in order:
        for j in range(per):
            arrive(dx, dz, j)

    for k in range(2):
        for s in range(SPLIT):
            far, near, mine = first(k, s)

            @pl.when(jnp.logical_not(mine))
            def _():
                far.wait_send()
    for copy in sends:
        copy.wait_send()
    for dx, dz in order:
        for j in range(per):
            each_halo(lambda side: halo(dx, dz, j, side).wait_send())

            @pl.when(o < 15)
            def _():
                halo(dx, dz, j, 0).wait_recv()

            @pl.when(o > 0)
            def _():
                halo(dx, dz, j, 1).wait_recv()


def gather_rows(x, levels, pad):
    per = 2 * SPLIT
    n_sends = 64 * SPLIT
    return pl.pallas_call(
        functools.partial(gather_kernel, levels, pad),
        out_shape=jax.ShapeDtypeStruct((4, 64, pad, 128), jnp.bfloat16),
        in_specs=[pl.BlockSpec(memory_space=pltpu.VMEM)],
        out_specs=pl.BlockSpec(memory_space=pl.ANY),
        scratch_shapes=[
            pltpu.VMEM((4, 4, pad, 128), jnp.bfloat16),
            pltpu.VMEM((8, pad, 128), jnp.bfloat16),
            pltpu.SemaphoreType.DMA((n_sends,)),
            pltpu.SemaphoreType.DMA((2, SPLIT)),
            pltpu.SemaphoreType.DMA((2, 4, per)),
            pltpu.SemaphoreType.DMA((2, 8 * per)),
            pltpu.SemaphoreType.DMA((2, 8 * per)),
            pltpu.SemaphoreType.DMA((8,)),
        ],
        compiler_params=pltpu.CompilerParams(
            collective_id=0, has_side_effects=True, vmem_limit_bytes=40 << 20
        ),
        cost_estimate=pl.CostEstimate(flops=0, bytes_accessed=20 << 20, transcendentals=0),
        name="gather_rows",
    )(x)


def band_kernel(levels, pad, weights_ref, offsets_ref, slots_ref, f_ref, filters_ref, vertical_ref, out_ref, blended, taps, vert, mixed):
    step = pl.program_id(0)
    me = lax.axis_index("lat")
    band = jnp.int32(0)
    for b in range(8):
        band = band + jnp.where(slots_ref[b] == me, b, 0)

    @pl.when(step == 0)
    def _():
        taps[...] = jnp.zeros_like(taps)
        for tap in range(-3, 4):
            total = jnp.zeros((128, 128), jnp.float32)
            for k in range(5):
                hit = (offsets_ref[band, k] == tap).astype(jnp.float32)
                total = total + hit * filters_ref[band, k].astype(jnp.float32)
            block = total.astype(jnp.bfloat16)
            for m in range(2):
                at = tap + 3 + m
                taps[at * 128 : (at + 1) * 128, m * 128 : (m + 1) * 128] = block
        chosen = lax.broadcasted_iota(jnp.int32, (levels, 8, levels), 1) == band
        picked = jnp.sum(jnp.where(chosen, vertical_ref[...].astype(jnp.float32), 0.0), axis=1)
        vert[...] = jnp.zeros_like(vert)
        vert[0:levels, 0:levels] = picked.astype(jnp.bfloat16)

    w0, w1, w2 = weights_ref[0, band], weights_ref[1, band], weights_ref[2, band]
    chunk = (step + 7) % 8

    def blend(q, carry):
        rows = [f_ref[i, q].astype(jnp.float32) for i in range(4)]
        for i in range(2):
            value = w0 * rows[i] + w1 * rows[i + 1] + w2 * rows[i + 2]
            blended[i, chunk * 8 + q] = value.astype(jnp.bfloat16)
        return carry

    lax.fori_loop(0, 8, blend, 0)

    @pl.when(step >= 2)
    def _():
        base = (step - 2) * 8
        for i in range(2):
            def pair(p, carry):
                q = base + 2 * p
                parts = [blended[i, (q + 61 + n) % 64] for n in range(8)]
                lhs = jnp.concatenate(parts, axis=1)
                smooth = jnp.dot(lhs, taps[...], preferred_element_type=jnp.float32).astype(jnp.bfloat16)
                result = jnp.dot(vert[...], smooth, preferred_element_type=jnp.float32)
                for m in range(2):
                    mixed[pl.ds(2 * p + m, pad, stride=8), :] = result[:, m * 128 : (m + 1) * 128]
                return carry

            lax.fori_loop(0, 4, pair, 0)
            flat = mixed[0 : levels * 8, :].astype(jnp.bfloat16)
            out_ref[i] = flat.reshape(levels, 8, 128)


def band_output(weights, offsets, slots, rows, filters, vertical, levels, pad):
    whole = lambda *shape: pl.BlockSpec(shape, lambda s, *_: (0,) * len(shape), pipeline_mode=pl.Buffered(1))
    return pl.pallas_call(
        functools.partial(band_kernel, levels, pad),
        out_shape=jax.ShapeDtypeStruct((2, levels, 64, 128), jnp.bfloat16),
        grid_spec=pltpu.PrefetchScalarGridSpec(
            num_scalar_prefetch=3,
            grid=(10,),
            in_specs=[
                pl.BlockSpec((4, 8, pad, 128), lambda s, *_: (0, (s + 7) % 8, 0, 0)),
                whole(8, 5, 128, 128),
                whole(levels, 8, levels),
            ],
            out_specs=pl.BlockSpec((2, levels, 8, 128), lambda s, *_: (0, 0, jnp.maximum(s - 2, 0), 0)),
            scratch_shapes=[
                pltpu.VMEM((2, 64, pad, 128), jnp.bfloat16),
                pltpu.VMEM((1024, 256), jnp.bfloat16),
                pltpu.VMEM((pad, pad), jnp.bfloat16),
                pltpu.VMEM((pad * 8, 128), jnp.float32),
            ],
        ),
        compiler_params=pltpu.CompilerParams(vmem_limit_bytes=48 << 20),
        name="band_output",
    )(weights, offsets, slots, rows, filters, vertical)


def on_device(grad_field, lat_weights, block_offsets, filters, vertical, slot_of_band):
    levels = grad_field.shape[2]
    pad = (levels + 15) // 16 * 16
    x = grad_field.transpose(0, 2, 1, 3).reshape(-1, 128)
    rows = gather_rows(x, levels, pad)
    out = band_output(
        lat_weights.T, block_offsets, slot_of_band, rows, filters, vertical.transpose(1, 0, 2), levels, pad
    )
    return out.transpose(0, 2, 1, 3)[None]


def solution(mesh):
    placed = (P("lat", "lon", None, None), P(), P(), P(), P(), P())
    return jax.shard_map(
        on_device,
        mesh=mesh,
        in_specs=placed,
        out_specs=P("lat", "lon", None, None, None),
        check_vma=False,
    )
```

```python
import functools

import jax
import jax.numpy as jnp
from jax import lax
from jax.experimental import pallas as pl
from jax.experimental.pallas import tpu as pltpu
from jax.sharding import PartitionSpec as P

MESH = pl.DeviceIdType.MESH
SPLIT = 2
LATE = 1


def fused_kernel(
    levels, pad,
    weights_ref, offsets_ref, slots_ref, x_hbm, filters_hbm, vertical_hbm, out_hbm,
    x_ref, filters_ref, vertical_ref, staged, shifted, rows_ref, blended, taps, vert, mixed, done,
    load_sems, send_sems, shift_sems, first_sems, recv_sems, halo_send, halo_recv, ready_sem, store_sems,
):
    o, t = lax.axis_index("lon"), lax.axis_index("lat")
    xh, z = t // 4, t % 4
    xl, y, core = o // 8, (o // 2) % 4, o % 2
    x = 2 * xh + xl
    zp, zm = xh * 4 + (z + 1) % 4, xh * 4 + (z + 3) % 4
    xp = (1 - xh) * 4 + z
    nq = 4 // SPLIT
    per = 2 * SPLIT
    half = 2 * levels * 4

    x_loads = [
        pltpu.make_async_copy(x_hbm.at[pl.ds(k * half, half)], x_ref.at[pl.ds(k * half, half)], load_sems.at[k])
        for k in range(2)
    ]
    weight_loads = [
        pltpu.make_async_copy(filters_hbm, filters_ref, load_sems.at[2]),
        pltpu.make_async_copy(vertical_hbm, vertical_ref, load_sems.at[3]),
    ]
    for load in x_loads:
        load.start()

    ahead = (y + 2 * core) % 4
    shift_to, shift_from = xh * 4 + (z + ahead) % 4, xh * 4 + (z + 4 - ahead) % 4
    stays = ahead == 0
    row_group = (z + 8 - y - 2 * core) % 4
    relay_lat = xl * 4 + z

    def relay_lon(k):
        return xh * 8 + row_group * 2 + k

    def source_lon(j):
        return xh * 8 + ((z + 8 - y - 2 * j) % 4) * 2 + j

    barrier = pltpu.get_barrier_semaphore()

    def greet(lon, lat):
        pl.semaphore_signal(barrier, inc=1, device_id={"lon": lon, "lat": lat}, device_id_type=MESH)

    greet(o, shift_to)
    greet(o, shift_from)
    for k in range(2):
        greet(relay_lon(k), relay_lat)
        greet(source_lon(k), relay_lat)
    for lat in (zp, zm, xp):
        greet(o, lat)
    peers = [(o, xh * 4 + (z + n) % 4) for n in (1, 2, 3)]
    peers += [(xl * 8 + ((y + n) % 4) * 2 + core, t) for n in (1, 2, 3)]
    peers += [(((x + n) % 2) * 8 + y * 2 + core, ((x + n) % 4) // 2 * 4 + z) for n in (1, 2, 3)]
    peers += [(o + 1 - 2 * core, t)]
    for lon, lat in peers:
        greet(lon, lat)

    def each_side(action):
        @pl.when(o > 0)
        def _():
            action(0)

        @pl.when(o < 15)
        def _():
            action(1)

    def crosses(side):
        return o == (8 if side == 0 else 7)

    def greet_side(side):
        greet(o - 1 + 2 * side, t)
        greet(o - 1 + 2 * side, jnp.where(crosses(side), xp, t))

    each_side(greet_side)

    def stage(k):
        for i in (2 * k, 2 * k + 1):
            for q in range(4):
                value = x_ref[pl.ds(i * levels * 4 + q, levels, stride=4), :]
                staged[i, q, 0:levels, :] = value.astype(jnp.bfloat16)
                staged[i, q, levels:pad, :] = jnp.zeros((pad - levels, 128), jnp.bfloat16)

    def shift(k, s, action):
        at = (pl.ds(2 * k, 2), pl.ds(s * nq, nq))
        src, dst = staged.at[at], shifted.at[at]

        @pl.when(stays)
        def _():
            if action == "start":
                pltpu.make_async_copy(src, dst, shift_sems.at[1, k, s]).start()

        @pl.when(jnp.logical_not(stays))
        def _():
            far = pltpu.make_async_remote_copy(
                src, dst, shift_sems.at[0, k, s], shift_sems.at[1, k, s],
                device_id={"lon": o, "lat": shift_to}, device_id_type=MESH,
            )
            if action == "start":
                far.start()
            else:
                far.wait_send()

    def first(k, s, action):
        src = shifted.at[pl.ds(2 * k, 2), pl.ds(s * nq, nq)]
        dst = rows_ref.at[pl.ds(1, 2), pl.ds(4 * o + s * nq, nq)]
        here = recv_sems.at[0, 0, core * SPLIT + s]
        mine = (relay_lat == t) & (relay_lon(k) == o)

        @pl.when(mine)
        def _():
            if action == "start":
                pltpu.make_async_copy(src, dst, here).start()

        @pl.when(jnp.logical_not(mine))
        def _():
            far = pltpu.make_async_remote_copy(
                src, dst, first_sems.at[k, s], here,
                device_id={"lon": relay_lon(k), "lat": relay_lat}, device_id_type=MESH,
            )
            if action == "start":
                far.start()
            else:
                far.wait_send()

    edge = (o == 0).astype(jnp.int32) + (o == 15).astype(jnp.int32)
    x_loads[0].wait()
    stage(0)
    pl.semaphore_wait(barrier, 23 - 2 * edge)
    parts = [(k, s) for s in range(SPLIT) for k in range(2)]
    for s in range(SPLIT):
        shift(0, s, "start")
    x_loads[1].wait()
    stage(1)
    for s in range(SPLIT):
        shift(1, s, "start")
    for load in weight_loads:
        load.start()

    for k, s in parts:
        dst = shifted.at[pl.ds(2 * k, 2), pl.ds(s * nq, nq)]
        pltpu.make_async_copy(dst, dst, shift_sems.at[1, k, s]).wait()
        first(k, s, "start")

    @pl.when(edge > 0)
    def _():
        row = jnp.where(o == 0, 0, 3)

        def fill(q, carry):
            rows_ref[row, q] = jnp.zeros((pad, 128), jnp.bfloat16)
            return carry

        lax.fori_loop(0, 64, fill, 0)

    band = jnp.int32(0)
    for b in range(8):
        band = jnp.where(slots_ref[b] == t, b, band)
    w0, w1, w2 = weights_ref[0, band], weights_ref[1, band], weights_ref[2, band]
    for load in weight_loads:
        load.wait()
    taps[...] = jnp.zeros_like(taps)
    for tap in range(-3, 4):
        total = jnp.zeros((128, 128), jnp.float32)
        for k in range(5):
            hit = (offsets_ref[band, k] == tap).astype(jnp.float32)
            total = total + hit * filters_ref[band, k].astype(jnp.float32)
        block = total.astype(jnp.bfloat16)
        for m in range(2):
            at = tap + 3 + m
            taps[at * 128 : (at + 1) * 128, m * 128 : (m + 1) * 128] = block
    chosen = lax.broadcasted_iota(jnp.int32, (levels, 8, levels), 1) == band
    picked = jnp.sum(jnp.where(chosen, vertical_ref[...].astype(jnp.float32), 0.0), axis=1)
    vert[...] = jnp.zeros_like(vert)
    vert[0:levels, 0:levels] = picked.astype(jnp.bfloat16)

    sends = []

    def block_of(dx, dz, j):
        return ((xh + dx) % 2) * 8 + ((z + dz + 8 - y - 2 * j) % 4) * 2 + j

    def rows_of(dx, dz, n):
        return pl.ds(block_of(dx, dz, n // SPLIT) * 4 + (n % SPLIT) * nq, nq)

    def piece(dx, dz, n):
        return rows_ref.at[pl.ds(1, 2), rows_of(dx, dz, n)]

    def send(dx, dz, n, to, there):
        ref = piece(dx, dz, n)
        copy = pltpu.make_async_remote_copy(
            ref, ref, send_sems.at[len(sends)], recv_sems.at[there[0], there[1], n],
            device_id={"lon": o, "lat": to}, device_id_type=MESH,
        )
        copy.start()
        sends.append(copy)

    def halo(dx, dz, n, side, partner=False):
        q = rows_of(dx, dz, n)
        src = rows_ref.at[1 + side, q]
        dst = rows_ref.at[3 - 3 * side, q]
        slot = block_of(dx, dz, n // SPLIT) * SPLIT + n % SPLIT
        own = block_of(dx + 1, dz, n // SPLIT) * SPLIT + n % SPLIT if partner else slot
        return pltpu.make_async_remote_copy(
            src, dst, halo_send.at[side, own], halo_recv.at[side, slot],
            device_id={"lon": o - 1 + 2 * side, "lat": xp if partner else t}, device_id_type=MESH,
        )

    def start_halo(dx, dz, n, side):
        if dx == 0:
            halo(dx, dz, n, side).start()

            @pl.when(crosses(side))
            def _():
                halo(dx, dz, n, side, True).start()
        else:
            @pl.when(jnp.logical_not(crosses(side)))
            def _():
                halo(dx, dz, n, side).start()

    def arrive(dx, dz, n):
        if (dx, dz) != (0, 0):
            ref = piece(dx, dz, n)
            pltpu.make_async_copy(ref, ref, recv_sems.at[dx, dz, n]).wait()
        late = n % SPLIT >= SPLIT - LATE
        ring = dx == 0 or not late
        if dx == 0 and dz == 0:
            send(dx, dz, n, xp, (1, 0))
        if ring and dz == 0:
            send(dx, dz, n, zp, (dx, 3))
            send(dx, dz, n, zm, (dx, 1))
        if ring and dz == 3 and n < per // 2:
            send(dx, dz, n, zp, (dx, 2))
        if ring and dz == 1 and n >= per // 2:
            send(dx, dz, n, zm, (dx, 2))
        if dx == 0 and dz != 0 and late:
            send(dx, dz, n, xp, (1, dz))
        each_side(lambda side: start_halo(dx, dz, n, side))

    def blend_block(block):
        for s in range(SPLIT):
            for side, present in ((1, o > 0), (0, o < 15)):

                @pl.when(present)
                def _():
                    dst = rows_ref.at[3 - 3 * side, pl.ds(block * 4 + s * nq, nq)]
                    pltpu.make_async_copy(dst, dst, halo_recv.at[side, block * SPLIT + s]).wait()

        for q in range(4):
            rows = [rows_ref[i, block * 4 + q].astype(jnp.float32) for i in range(4)]
            m = (2 * block + (q + 1) // 2) % 32
            for i in range(2):
                value = w0 * rows[i] + w1 * rows[i + 1] + w2 * rows[i + 2]
                blended[i, m, 1 - q % 2] = value.astype(jnp.bfloat16)

    def blend_group(group):
        def body(n, carry):
            blend_block(group * 8 + n)
            return carry

        lax.fori_loop(0, 8, body, 0)

    def store(slot, chunk):
        return pltpu.make_async_copy(
            done.at[slot], out_hbm.at[pl.ds(0, 2), pl.ds(0, levels), pl.ds(pl.multiple_of(chunk * 8, 8), 8)], store_sems.at[slot]
        )

    def chunk_output(chunk, slot):
        for i in range(2):
            blocks = []
            for n in range(7):
                m = (chunk * 4 + n + 31) % 32
                blocks.append(jnp.concatenate([blended[i, m, 0], blended[i, m, 1]], axis=1))
            lhs = jnp.concatenate([jnp.concatenate(blocks[k : k + 4], axis=0) for k in range(4)], axis=1)
            smooth = jnp.dot(lhs, taps[...], preferred_element_type=jnp.float32).astype(jnp.bfloat16)
            wide = jnp.concatenate([smooth[p * pad : (p + 1) * pad] for p in range(4)], axis=1)
            result = jnp.dot(vert[...], wide, preferred_element_type=jnp.float32)
            for n in range(8):
                mixed[pl.ds(n, pad, stride=8), :] = result[:, n * 128 : (n + 1) * 128]
            flat = mixed[0 : levels * 8, :].reshape(levels, 8, 128)
            done[slot, i] = flat.astype(jnp.bfloat16)
        store(slot, chunk).start()

    def outputs(count, first_chunk):
        def body(n, carry):
            chunk = (first_chunk + n) % 8

            @pl.when(n >= 2)
            def _():
                store(n % 2, chunk).wait()

            chunk_output(chunk, n % 2)
            return carry

        lax.fori_loop(0, count, body, 0)
        for slot in range(2):
            store(slot, 0).wait()

    for n in range(per):
        ref = piece(0, 0, n)
        pltpu.make_async_copy(ref, ref, recv_sems.at[0, 0, n]).wait()
    for lon, lat in peers:
        pl.semaphore_signal(ready_sem, inc=1, device_id={"lon": lon, "lat": lat}, device_id_type=MESH)
    pl.semaphore_wait(ready_sem, 10)

    everything = range(per)
    late = [n for n in everything if n % SPLIT >= SPLIT - LATE]
    early = [n for n in everything if n not in late]
    for dx, dz, which in ORDER_1:
        for n in {"all": everything, "late": late, "early": early}[which]:
            arrive(dx, dz, n)
    blend_group(xh)
    outputs(2, 4 * xh + 1)
    for dx, dz, which in ORDER_2:
        for n in {"all": everything, "late": late, "early": early}[which]:
            arrive(dx, dz, n)
    blend_group(1 - xh)
    outputs(6, 4 * xh + 3)

    for k, s in parts:
        shift(k, s, "wait")
        first(k, s, "wait")
    for copy in sends:
        copy.wait_send()
    for dx in range(2):
        for dz in range(4):
            for n in range(per):
                each_side(lambda side: halo(dx, dz, n, side).wait_send())


ORDER_1 = [(0, 0, "all"), (0, 1, "all"), (0, 3, "all"), (1, 0, "all"), (0, 2, "all"), (1, 1, "early"), (1, 3, "early")]
ORDER_2 = [(1, 2, "early"), (1, 1, "late"), (1, 3, "late"), (1, 2, "late")]


def fused(weights, offsets, slots, x, filters, vertical, levels, pad):
    per = 2 * SPLIT
    smem, anywhere = pl.BlockSpec(memory_space=pltpu.SMEM), pl.BlockSpec(memory_space=pl.ANY)
    return pl.pallas_call(
        functools.partial(fused_kernel, levels, pad),
        out_shape=jax.ShapeDtypeStruct((2, levels, 64, 128), jnp.bfloat16),
        in_specs=[smem, smem, smem, anywhere, anywhere, anywhere],
        out_specs=anywhere,
        scratch_shapes=[
            pltpu.VMEM((16 * levels, 128), jnp.float32),
            pltpu.VMEM((8, 5, 128, 128), jnp.bfloat16),
            pltpu.VMEM((levels, 8, levels), jnp.bfloat16),
            pltpu.VMEM((4, 4, pad, 128), jnp.bfloat16),
            pltpu.VMEM((4, 4, pad, 128), jnp.bfloat16),
            pltpu.VMEM((4, 64, pad, 128), jnp.bfloat16),
            pltpu.VMEM((2, 32, 2, pad, 128), jnp.bfloat16),
            pltpu.VMEM((1024, 256), jnp.bfloat16),
            pltpu.VMEM((pad, pad), jnp.bfloat16),
            pltpu.VMEM((pad * 8, 128), jnp.float32),
            pltpu.VMEM((2, 2, levels, 8, 128), jnp.bfloat16),
            pltpu.SemaphoreType.DMA((4,)),
            pltpu.SemaphoreType.DMA((32 * SPLIT,)),
            pltpu.SemaphoreType.DMA((2, 2, SPLIT)),
            pltpu.SemaphoreType.DMA((2, SPLIT)),
            pltpu.SemaphoreType.DMA((2, 4, per)),
            pltpu.SemaphoreType.DMA((2, 8 * per)),
            pltpu.SemaphoreType.DMA((2, 8 * per)),
            pltpu.SemaphoreType.REGULAR,
            pltpu.SemaphoreType.DMA((2,)),
        ],
        compiler_params=pltpu.CompilerParams(
            collective_id=0, has_side_effects=True, vmem_limit_bytes=VMEM_MIB << 20
        ),
        name="fused",
    )(weights, offsets, slots, x, filters, vertical)


VMEM_MIB = 60


def on_device(grad_field, lat_weights, block_offsets, filters, vertical, slot_of_band):
    levels = grad_field.shape[2]
    pad = (levels + 15) // 16 * 16
    x = grad_field.transpose(0, 2, 1, 3).reshape(-1, 128)
    out = fused(
        lat_weights.T, block_offsets, slot_of_band, x, filters, vertical.transpose(1, 0, 2), levels, pad
    )
    return out.transpose(0, 2, 1, 3)[None]


def solution(mesh):
    placed = (P("lat", "lon", None, None), P(), P(), P(), P(), P())
    return jax.shard_map(
        on_device,
        mesh=mesh,
        in_specs=placed,
        out_specs=P("lat", "lon", None, None, None),
        check_vma=False,
    )
```

```python
import functools

import jax
import jax.numpy as jnp
from jax import lax
from jax.experimental import pallas as pl
from jax.experimental.pallas import tpu as pltpu
from jax.sharding import PartitionSpec as P

MESH = pl.DeviceIdType.MESH
SPLIT = 2
LATE = (1,)


def chunk_output(chunk, slot, taps, vert, mixed, load_pair, done):
    levels, pad = done.shape[-3], vert.shape[0]
    for i in range(2):
        pairs = [load_pair(i, chunk * 4 + n + 31) for n in range(7)]
        lhs = jnp.concatenate([jnp.concatenate(pairs[k : k + 4], axis=0) for k in range(4)], axis=1)
        smooth = jnp.dot(lhs, taps[...], preferred_element_type=jnp.float32).astype(jnp.bfloat16)
        wide = jnp.concatenate([smooth[p * pad : (p + 1) * pad] for p in range(4)], axis=1)
        result = jnp.dot(vert[...], wide, preferred_element_type=jnp.float32)
        for n in range(8):
            mixed[i, pl.ds(n, pad, stride=8), :] = result[:, n * 128 : (n + 1) * 128]
        flat = mixed[i, 0 : levels * 8, :].reshape(levels, 8, 128)
        done[slot, i] = flat.astype(jnp.bfloat16)


def outer_kernel(before_ref, here_ref, after_ref, inner_ref, taps_ref, vert_ref, out_ref, mixed):
    chunk = pl.program_id(0)
    ready = chunk - 4 * (lax.axis_index("lat") // 4) - 1
    inner = (ready >= 0) & (ready < 2)

    def load_pair(i, n):
        ref, m = ((before_ref, 3), *((here_ref, k) for k in range(4)), (after_ref, 0), (after_ref, 1))[n - 31]
        return jnp.concatenate([ref[i, m, 0], ref[i, m, 1]], axis=1)

    @pl.when(inner)
    def _():
        out_ref[...] = inner_ref[...]

    @pl.when(jnp.logical_not(inner))
    def _():
        chunk_output(0, 0, taps_ref, vert_ref, mixed, load_pair, out_ref)


def outer_outputs(blended, inner, taps, vert, levels, pad):
    def pairs(shift):
        return pl.BlockSpec((2, 4, 2, pad, 128), lambda c: (0, (c + shift) % 8, 0, 0, 0))

    return pl.pallas_call(
        outer_kernel,
        out_shape=jax.ShapeDtypeStruct((1, 2, levels, 64, 128), jnp.bfloat16),
        grid=(8,),
        in_specs=[
            pairs(7), pairs(0), pairs(1),
            pl.BlockSpec((1, 2, levels, 8, 128), lambda c: (jnp.clip(c % 4 - 1, 0, 1), 0, 0, 0, 0)),
            pl.BlockSpec((1024, 256), lambda c: (0, 0)),
            pl.BlockSpec((pad, pad), lambda c: (0, 0)),
        ],
        out_specs=pl.BlockSpec((1, 2, levels, 8, 128), lambda c: (0, 0, 0, c, 0)),
        scratch_shapes=[pltpu.VMEM((2, pad * 8, 128), jnp.float32)],
        compiler_params=pltpu.CompilerParams(vmem_limit_bytes=OUTER_MIB << 20),
        name="outer_outputs",
    )(blended, blended, blended, inner, taps, vert)


def fused_kernel(
    levels, pad,
    weights_ref, offsets_ref, slots_ref, x_hbm, filters_hbm, vertical_hbm,
    blended_hbm, inner_hbm, taps_hbm, vert_hbm,
    x_ref, filters_ref, vertical_ref, staged, shifted, rows_ref, blended, taps, vert, mixed, done,
    load_sems, send_sems, shift_sems, first_sems, recv_sems, halo_send, halo_recv, ready_sem, store_sems, out_sems, table_sems,
):
    o, t = lax.axis_index("lon"), lax.axis_index("lat")
    xh, z = t // 4, t % 4
    xl, y, core = o // 8, (o // 2) % 4, o % 2
    x = 2 * xh + xl
    zp, zm = xh * 4 + (z + 1) % 4, xh * 4 + (z + 3) % 4
    xp = (1 - xh) * 4 + z
    nq = 4 // SPLIT
    per = 2 * SPLIT
    half = 2 * levels * 4

    x_loads = [
        pltpu.make_async_copy(x_hbm.at[pl.ds(k * half, half)], x_ref.at[pl.ds(k * half, half)], load_sems.at[k])
        for k in range(2)
    ]
    weight_loads = [
        pltpu.make_async_copy(filters_hbm, filters_ref, load_sems.at[2]),
        pltpu.make_async_copy(vertical_hbm, vertical_ref, load_sems.at[3]),
    ]
    for load in x_loads:
        load.start()

    ahead = (y + 2 * core) % 4
    shift_to, shift_from = xh * 4 + (z + ahead) % 4, xh * 4 + (z + 4 - ahead) % 4
    stays = ahead == 0
    row_group = (z + 8 - y - 2 * core) % 4
    relay_lat = xl * 4 + z

    def relay_lon(k):
        return xh * 8 + row_group * 2 + k

    def source_lon(j):
        return xh * 8 + ((z + 8 - y - 2 * j) % 4) * 2 + j

    barrier = pltpu.get_barrier_semaphore()

    def greet(lon, lat):
        pl.semaphore_signal(barrier, inc=1, device_id={"lon": lon, "lat": lat}, device_id_type=MESH)

    greet(o, shift_to)
    greet(o, shift_from)
    for k in range(2):
        greet(relay_lon(k), relay_lat)
        greet(source_lon(k), relay_lat)
    for lat in (zp, zm, xp):
        greet(o, lat)
    peers = [(o, xh * 4 + (z + n) % 4) for n in (1, 2, 3)]
    peers += [(xl * 8 + ((y + n) % 4) * 2 + core, t) for n in (1, 2, 3)]
    peers += [(((x + n) % 2) * 8 + y * 2 + core, ((x + n) % 4) // 2 * 4 + z) for n in (1, 2, 3)]
    peers += [(o + 1 - 2 * core, t)]
    for lon, lat in peers:
        greet(lon, lat)

    def each_side(action):
        @pl.when(o > 0)
        def _():
            action(0)

        @pl.when(o < 15)
        def _():
            action(1)

    def crosses(side):
        return o == (8 if side == 0 else 7)

    def greet_side(side):
        greet(o - 1 + 2 * side, t)
        greet(o - 1 + 2 * side, jnp.where(crosses(side), xp, t))

    each_side(greet_side)

    def stage(k):
        for i in (2 * k, 2 * k + 1):
            for q in range(4):
                value = x_ref[pl.ds(i * levels * 4 + q, levels, stride=4), :]
                staged[i, q, 0:levels, :] = value.astype(jnp.bfloat16)
                staged[i, q, levels:pad, :] = jnp.zeros((pad - levels, 128), jnp.bfloat16)

    def shift(k, s, action):
        at = (pl.ds(2 * k, 2), pl.ds(s * nq, nq))
        src, dst = staged.at[at], shifted.at[at]

        @pl.when(stays)
        def _():
            if action == "start":
                pltpu.make_async_copy(src, dst, shift_sems.at[1, k, s]).start()

        @pl.when(jnp.logical_not(stays))
        def _():
            far = pltpu.make_async_remote_copy(
                src, dst, shift_sems.at[0, k, s], shift_sems.at[1, k, s],
                device_id={"lon": o, "lat": shift_to}, device_id_type=MESH,
            )
            if action == "start":
                far.start()
            else:
                far.wait_send()

    def first(k, s, action):
        src = shifted.at[pl.ds(2 * k, 2), pl.ds(s * nq, nq)]
        dst = rows_ref.at[pl.ds(1, 2), pl.ds(4 * o + s * nq, nq)]
        here = recv_sems.at[0, 0, core * SPLIT + s]
        mine = (relay_lat == t) & (relay_lon(k) == o)

        @pl.when(mine)
        def _():
            if action == "start":
                pltpu.make_async_copy(src, dst, here).start()

        @pl.when(jnp.logical_not(mine))
        def _():
            far = pltpu.make_async_remote_copy(
                src, dst, first_sems.at[k, s], here,
                device_id={"lon": relay_lon(k), "lat": relay_lat}, device_id_type=MESH,
            )
            if action == "start":
                far.start()
            else:
                far.wait_send()

    edge = (o == 0).astype(jnp.int32) + (o == 15).astype(jnp.int32)
    x_loads[0].wait()
    stage(0)
    pl.semaphore_wait(barrier, 23 - 2 * edge)
    parts = [(k, s) for s in range(SPLIT) for k in range(2)]
    for s in range(SPLIT):
        shift(0, s, "start")
    x_loads[1].wait()
    stage(1)
    for s in range(SPLIT):
        shift(1, s, "start")
    for load in weight_loads:
        load.start()

    for k, s in parts:
        dst = shifted.at[pl.ds(2 * k, 2), pl.ds(s * nq, nq)]
        pltpu.make_async_copy(dst, dst, shift_sems.at[1, k, s]).wait()
        first(k, s, "start")

    @pl.when(edge > 0)
    def _():
        row = jnp.where(o == 0, 0, 3)

        def fill(q, carry):
            rows_ref[row, q] = jnp.zeros((pad, 128), jnp.bfloat16)
            return carry

        lax.fori_loop(0, 64, fill, 0)

    band = jnp.int32(0)
    for b in range(8):
        band = jnp.where(slots_ref[b] == t, b, band)
    w0, w1, w2 = weights_ref[0, band], weights_ref[1, band], weights_ref[2, band]
    for load in weight_loads:
        load.wait()
    taps[...] = jnp.zeros_like(taps)
    for tap in range(-3, 4):
        total = jnp.zeros((128, 128), jnp.float32)
        for k in range(5):
            hit = (offsets_ref[band, k] == tap).astype(jnp.float32)
            total = total + hit * filters_ref[band, k].astype(jnp.float32)
        block = total.astype(jnp.bfloat16)
        for m in range(2):
            at = tap + 3 + m
            taps[at * 128 : (at + 1) * 128, m * 128 : (m + 1) * 128] = block
    chosen = lax.broadcasted_iota(jnp.int32, (levels, 8, levels), 1) == band
    picked = jnp.sum(jnp.where(chosen, vertical_ref[...].astype(jnp.float32), 0.0), axis=1)
    vert[...] = jnp.zeros_like(vert)
    vert[0:levels, 0:levels] = picked.astype(jnp.bfloat16)

    tables = [
        pltpu.make_async_copy(taps, taps_hbm, table_sems.at[0]),
        pltpu.make_async_copy(vert, vert_hbm, table_sems.at[1]),
    ]
    for table in tables:
        table.start()

    sends = []

    def block_of(dx, dz, j):
        return ((xh + dx) % 2) * 8 + ((z + dz + 8 - y - 2 * j) % 4) * 2 + j

    def rows_of(dx, dz, n):
        return pl.ds(block_of(dx, dz, n // SPLIT) * 4 + (n % SPLIT) * nq, nq)

    def piece(dx, dz, n):
        return rows_ref.at[pl.ds(1, 2), rows_of(dx, dz, n)]

    def send(dx, dz, n, to, there):
        ref = piece(dx, dz, n)
        copy = pltpu.make_async_remote_copy(
            ref, ref, send_sems.at[len(sends)], recv_sems.at[there[0], there[1], n],
            device_id={"lon": o, "lat": to}, device_id_type=MESH,
        )
        copy.start()
        sends.append(copy)

    def halo(dx, dz, n, side, partner=False):
        q = rows_of(dx, dz, n)
        src = rows_ref.at[1 + side, q]
        dst = rows_ref.at[3 - 3 * side, q]
        slot = block_of(dx, dz, n // SPLIT) * SPLIT + n % SPLIT
        own = block_of(dx + 1, dz, n // SPLIT) * SPLIT + n % SPLIT if partner else slot
        return pltpu.make_async_remote_copy(
            src, dst, halo_send.at[side, own], halo_recv.at[side, slot],
            device_id={"lon": o - 1 + 2 * side, "lat": xp if partner else t}, device_id_type=MESH,
        )

    def start_halo(dx, dz, n, side):
        if dx == 0:
            halo(dx, dz, n, side).start()

            @pl.when(crosses(side))
            def _():
                halo(dx, dz, n, side, True).start()
        else:
            @pl.when(jnp.logical_not(crosses(side)))
            def _():
                halo(dx, dz, n, side).start()

    def arrive(dx, dz, n):
        if (dx, dz) != (0, 0):
            ref = piece(dx, dz, n)
            pltpu.make_async_copy(ref, ref, recv_sems.at[dx, dz, n]).wait()
        late = n in LATE
        ring = dx == 0 or not late
        if dx == 0 and dz == 0:
            send(dx, dz, n, xp, (1, 0))
        if ring and dz == 0:
            send(dx, dz, n, zp, (dx, 3))
            send(dx, dz, n, zm, (dx, 1))
        if ring and dz == 3 and n < per // 2:
            send(dx, dz, n, zp, (dx, 2))
        if ring and dz == 1 and n >= per // 2:
            send(dx, dz, n, zm, (dx, 2))
        if dx == 0 and dz != 0 and late:
            send(dx, dz, n, xp, (1, dz))
        each_side(lambda side: start_halo(dx, dz, n, side))

    def blend_block(block):
        for s in range(SPLIT):
            for side, present in ((1, o > 0), (0, o < 15)):

                @pl.when(present)
                def _():
                    dst = rows_ref.at[3 - 3 * side, pl.ds(block * 4 + s * nq, nq)]
                    pltpu.make_async_copy(dst, dst, halo_recv.at[side, block * SPLIT + s]).wait()

        for q in range(4):
            rows = [rows_ref[i, block * 4 + q].astype(jnp.float32) for i in range(4)]
            m = (2 * block + (q + 1) // 2) % 32
            for i in range(2):
                value = w0 * rows[i] + w1 * rows[i + 1] + w2 * rows[i + 2]
                blended[i, m, 1 - q % 2] = value.astype(jnp.bfloat16)

    def keep(n, count, first):
        part = pl.ds(0, 2), pl.ds(first, count)
        return pltpu.make_async_copy(blended.at[part], blended_hbm.at[part], out_sems.at[n])

    def blend_own(n, carry):
        block = xh * 8 + n
        blend_block(block)

        @pl.when(n == 0)
        def _():
            keep(n, 1, 2 * block + 1).start()

        @pl.when(n > 0)
        def _():
            keep(n, 2, 2 * block).start()

        return carry

    def blend_other(n, carry):
        block = (1 - xh) * 8 + n
        blend_block(block)
        keep(8 + n, 2, 2 * block).start()
        return carry

    def inner_outputs():
        def body(n, carry):
            chunk_output(4 * xh + 1 + n, n, taps, vert, mixed, lambda i, m: load_pair(i, m % 32), done)
            pltpu.make_async_copy(done.at[n], inner_hbm.at[n], store_sems.at[n]).start()
            return carry

        lax.fori_loop(0, 2, body, 0)

    def load_pair(i, m):
        return jnp.concatenate([blended[i, m, 0], blended[i, m, 1]], axis=1)

    for n in range(per):
        ref = piece(0, 0, n)
        pltpu.make_async_copy(ref, ref, recv_sems.at[0, 0, n]).wait()
    for lon, lat in peers:
        pl.semaphore_signal(ready_sem, inc=1, device_id={"lon": lon, "lat": lat}, device_id_type=MESH)
    pl.semaphore_wait(ready_sem, 10)

    everything = range(per)
    late = [n for n in everything if n in LATE]
    early = [n for n in everything if n not in late]
    for dx, dz, which in ORDER_1:
        for n in {"all": everything, "late": late, "early": early}[which]:
            arrive(dx, dz, n)
    lax.fori_loop(0, 8, blend_own, 0)
    for dx, dz, which in ORDER_2:
        for n in {"all": everything, "late": late, "early": early}[which]:
            arrive(dx, dz, n)
    inner_outputs()
    lax.fori_loop(0, 8, blend_other, 0)
    keep(16, 1, 16 * xh).start()

    for table in tables:
        table.wait()
    for n in range(2):
        pltpu.make_async_copy(done.at[n], inner_hbm.at[n], store_sems.at[n]).wait()
    for n in range(17):
        keep(n, 1 if n in (0, 16) else 2, 0).wait()
    for k, s in parts:
        shift(k, s, "wait")
        first(k, s, "wait")
    for copy in sends:
        copy.wait_send()
    for dx in range(2):
        for dz in range(4):
            for n in range(per):
                each_side(lambda side: halo(dx, dz, n, side).wait_send())


ORDER_1 = [(0, 0, "all"), (0, 1, "all"), (0, 3, "all"), (1, 0, "all"), (0, 2, "all"), (1, 1, "early"), (1, 3, "early")]
ORDER_2 = [(1, 2, "early"), (1, 1, "late"), (1, 3, "late"), (1, 2, "late")]


def fused(weights, offsets, slots, x, filters, vertical, levels, pad):
    per = 2 * SPLIT
    smem, anywhere = pl.BlockSpec(memory_space=pltpu.SMEM), pl.BlockSpec(memory_space=pl.ANY)
    return pl.pallas_call(
        functools.partial(fused_kernel, levels, pad),
        out_shape=[
            jax.ShapeDtypeStruct((2, 32, 2, pad, 128), jnp.bfloat16),
            jax.ShapeDtypeStruct((2, 2, levels, 8, 128), jnp.bfloat16),
            jax.ShapeDtypeStruct((1024, 256), jnp.bfloat16),
            jax.ShapeDtypeStruct((pad, pad), jnp.bfloat16),
        ],
        in_specs=[smem, smem, smem, anywhere, anywhere, anywhere],
        out_specs=[anywhere] * 4,
        scratch_shapes=[
            pltpu.VMEM((16 * levels, 128), jnp.float32),
            pltpu.VMEM((8, 5, 128, 128), jnp.bfloat16),
            pltpu.VMEM((levels, 8, levels), jnp.bfloat16),
            pltpu.VMEM((4, 4, pad, 128), jnp.bfloat16),
            pltpu.VMEM((4, 4, pad, 128), jnp.bfloat16),
            pltpu.VMEM((4, 64, pad, 128), jnp.bfloat16),
            pltpu.VMEM((2, 32, 2, pad, 128), jnp.bfloat16),
            pltpu.VMEM((1024, 256), jnp.bfloat16),
            pltpu.VMEM((pad, pad), jnp.bfloat16),
            pltpu.VMEM((2, pad * 8, 128), jnp.float32),
            pltpu.VMEM((2, 2, levels, 8, 128), jnp.bfloat16),
            pltpu.SemaphoreType.DMA((4,)),
            pltpu.SemaphoreType.DMA((32 * SPLIT,)),
            pltpu.SemaphoreType.DMA((2, 2, SPLIT)),
            pltpu.SemaphoreType.DMA((2, SPLIT)),
            pltpu.SemaphoreType.DMA((2, 4, per)),
            pltpu.SemaphoreType.DMA((2, 8 * per)),
            pltpu.SemaphoreType.DMA((2, 8 * per)),
            pltpu.SemaphoreType.REGULAR,
            pltpu.SemaphoreType.DMA((2,)),
            pltpu.SemaphoreType.DMA((17,)),
            pltpu.SemaphoreType.DMA((2,)),
        ],
        compiler_params=pltpu.CompilerParams(
            collective_id=0, has_side_effects=True, vmem_limit_bytes=VMEM_MIB << 20
        ),
        name="fused",
    )(weights, offsets, slots, x, filters, vertical)


VMEM_MIB = 60
OUTER_MIB = 60


def on_device(grad_field, lat_weights, block_offsets, filters, vertical, slot_of_band):
    levels = grad_field.shape[2]
    pad = (levels + 15) // 16 * 16
    x = grad_field.transpose(0, 2, 1, 3).reshape(-1, 128)
    blended, inner, taps, vert = fused(
        lat_weights.T, block_offsets, slot_of_band, x, filters, vertical.transpose(1, 0, 2), levels, pad
    )
    out = outer_outputs(blended, inner, taps, vert, levels, pad)
    return out.transpose(0, 1, 3, 2, 4)


def solution(mesh):
    placed = (P("lat", "lon", None, None), P(), P(), P(), P(), P())
    return jax.shard_map(
        on_device,
        mesh=mesh,
        in_specs=placed,
        out_specs=P("lat", "lon", None, None, None),
        check_vma=False,
    )
```

```python
import functools

import jax
import jax.numpy as jnp
from jax import lax
from jax.experimental import pallas as pl
from jax.experimental.pallas import tpu as pltpu
from jax.sharding import PartitionSpec as P

MESH = pl.DeviceIdType.MESH
SPLIT = 2
LATE = (1,)


def chunk_output(chunk, slot, taps, vert, mixed, load_pair, done):
    levels, pad = done.shape[-3], vert.shape[0]
    lhs = []
    for i in range(2):
        pairs = [load_pair(i, chunk * 4 + n + 31) for n in range(7)]
        lhs.append(jnp.concatenate([jnp.concatenate(pairs[k : k + 4], axis=0) for k in range(4)], axis=1))
    lhs = jnp.concatenate(lhs, axis=0)
    smooth = jnp.dot(lhs, taps[...], preferred_element_type=jnp.float32).astype(jnp.bfloat16)
    wide = jnp.concatenate([smooth[p * pad : (p + 1) * pad] for p in range(8)], axis=1)
    result = jnp.dot(vert[...], wide, preferred_element_type=jnp.float32)
    for i in range(2):
        for n in range(8):
            at = (8 * i + n) * 128
            mixed[i, pl.ds(n, pad, stride=8), :] = result[:, at : at + 128]
        flat = mixed[i, 0 : levels * 8, :].reshape(levels, 8, 128)
        done[slot, i] = flat.astype(jnp.bfloat16)


def outer_kernel(levels, blended_hbm, inner_hbm, taps_hbm, vert_hbm, out_hbm, blended, taps, vert, mixed, done, ready, load_sems, inner_sems, store_sems):
    xh = lax.axis_index("lat") // 4

    def group(k):
        part = pl.ds(0, 2), pl.ds(((4 * xh + 2 + k) % 8) * 4, 4)
        return pltpu.make_async_copy(blended_hbm.at[part], blended.at[part], load_sems.at[k])

    def place(chunk):
        return out_hbm.at[0, pl.ds(0, 2), pl.ds(0, levels), pl.ds(pl.multiple_of(chunk * 8, 8), 8)]

    def store(slot, chunk):
        return pltpu.make_async_copy(done.at[slot], place(chunk), store_sems.at[slot])

    tables = [
        pltpu.make_async_copy(taps_hbm, taps, load_sems.at[8]),
        pltpu.make_async_copy(vert_hbm, vert, load_sems.at[9]),
    ]
    loads = [pltpu.make_async_copy(inner_hbm.at[n], ready.at[n], inner_sems.at[n]) for n in range(2)]
    inner = [pltpu.make_async_copy(ready.at[n], place(4 * xh + 1 + n), inner_sems.at[2 + n]) for n in range(2)]
    for k in range(3):
        group(k).start()
    for copy in tables:
        copy.start()
    for k in range(3, 8):
        group(k).start()
    for copy in loads:
        copy.start()
    for k in range(2):
        group(k).wait()
    for copy in tables:
        copy.wait()

    def load_pair(i, m):
        return jnp.concatenate([blended[i, m % 32, 0], blended[i, m % 32, 1]], axis=1)

    def body(n, carry):
        group(n + 2).wait()
        chunk = (4 * xh + 3 + n) % 8

        @pl.when(n >= 2)
        def _():
            store(n % 2, chunk).wait()

        chunk_output(chunk, n % 2, taps, vert, mixed, load_pair, done)
        store(n % 2, chunk).start()

        @pl.when(n == 2)
        def _():
            for load, copy in zip(loads, inner):
                load.wait()
                copy.start()

        return carry

    lax.fori_loop(0, 6, body, 0)
    for slot in range(2):
        store(slot, 0).wait()
    for copy in inner:
        copy.wait()


def outer_outputs(blended, inner, taps, vert, levels, pad):
    anywhere = pl.BlockSpec(memory_space=pl.ANY)
    return pl.pallas_call(
        functools.partial(outer_kernel, levels),
        out_shape=jax.ShapeDtypeStruct((1, 2, levels, 64, 128), jnp.bfloat16),
        in_specs=[anywhere] * 4,
        out_specs=anywhere,
        scratch_shapes=[
            pltpu.VMEM((2, 32, 2, pad, 128), jnp.bfloat16),
            pltpu.VMEM((1024, 256), jnp.bfloat16),
            pltpu.VMEM((pad, pad), jnp.bfloat16),
            pltpu.VMEM((2, pad * 8, 128), jnp.float32),
            pltpu.VMEM((2, 2, levels, 8, 128), jnp.bfloat16),
            pltpu.VMEM((2, 2, levels, 8, 128), jnp.bfloat16),
            pltpu.SemaphoreType.DMA((10,)),
            pltpu.SemaphoreType.DMA((4,)),
            pltpu.SemaphoreType.DMA((2,)),
        ],
        compiler_params=pltpu.CompilerParams(vmem_limit_bytes=OUTER_MIB << 20),
        name="outer_outputs",
    )(blended, inner, taps, vert)


def fused_kernel(
    levels, pad,
    weights_ref, offsets_ref, slots_ref, x_hbm, filters_hbm, vertical_hbm,
    blended_hbm, inner_hbm, taps_hbm, vert_hbm,
    x_ref, filters_ref, vertical_ref, staged, shifted, rows_ref, blended, taps, vert, mixed, done,
    load_sems, send_sems, shift_sems, first_sems, recv_sems, halo_send, halo_recv, ready_sem, store_sems, out_sems, table_sems,
):
    o, t = lax.axis_index("lon"), lax.axis_index("lat")
    xh, z = t // 4, t % 4
    xl, y, core = o // 8, (o // 2) % 4, o % 2
    x = 2 * xh + xl
    zp, zm = xh * 4 + (z + 1) % 4, xh * 4 + (z + 3) % 4
    xp = (1 - xh) * 4 + z
    nq = 4 // SPLIT
    per = 2 * SPLIT
    half = 2 * levels * 4

    x_loads = [
        pltpu.make_async_copy(x_hbm.at[pl.ds(k * half, half)], x_ref.at[pl.ds(k * half, half)], load_sems.at[k])
        for k in range(2)
    ]
    weight_loads = [
        pltpu.make_async_copy(filters_hbm, filters_ref, load_sems.at[2]),
        pltpu.make_async_copy(vertical_hbm, vertical_ref, load_sems.at[3]),
    ]
    for load in x_loads:
        load.start()

    ahead = (y + 2 * core) % 4
    row_group = (z + 8 - y - 2 * core) % 4
    swapped = xh * 8 + y * 2 + core

    def shift_to(k):
        return (swapped, xl * 4 + (z + ahead) % 4) if k == 0 else (o, xh * 4 + (z + ahead) % 4)

    def shift_from(k):
        return (swapped, xl * 4 + (z + 4 - ahead) % 4) if k == 0 else (o, xh * 4 + (z + 4 - ahead) % 4)

    def stays(k):
        return (ahead == 0) & (xh == xl) if k == 0 else ahead == 0

    def relay(k):
        return (xl * 8 + row_group * 2, t) if k == 0 else (xh * 8 + row_group * 2 + 1, xl * 4 + z)

    def source(j):
        place = ((z + 8 - y - 2 * j) % 4) * 2 + j
        return jnp.where(core == 0, xl, xh) * 8 + place, jnp.where(core == 0, t, xl * 4 + z)

    barrier = pltpu.get_barrier_semaphore()

    def greet(lon, lat):
        pl.semaphore_signal(barrier, inc=1, device_id={"lon": lon, "lat": lat}, device_id_type=MESH)

    for k in range(2):
        greet(*shift_to(k))
        greet(*shift_from(k))
        greet(*relay(k))
        greet(*source(k))
    for lat in (zp, zm, xp):
        greet(o, lat)
    peers = [(o, xh * 4 + (z + n) % 4) for n in (1, 2, 3)]
    peers += [(xl * 8 + ((y + n) % 4) * 2 + core, t) for n in (1, 2, 3)]
    peers += [(((x + n) % 2) * 8 + y * 2 + core, ((x + n) % 4) // 2 * 4 + z) for n in (1, 2, 3)]
    peers += [(o + 1 - 2 * core, t)]
    for lon, lat in peers:
        greet(lon, lat)

    def each_side(action):
        @pl.when(o > 0)
        def _():
            action(0)

        @pl.when(o < 15)
        def _():
            action(1)

    def crosses(side):
        return o == (8 if side == 0 else 7)

    def greet_side(side):
        greet(o - 1 + 2 * side, t)
        greet(o - 1 + 2 * side, jnp.where(crosses(side), xp, t))

    each_side(greet_side)

    def stage(k):
        for i in (2 * k, 2 * k + 1):
            for q in range(4):
                value = x_ref[pl.ds(i * levels * 4 + q, levels, stride=4), :]
                staged[i, q, 0:levels, :] = value.astype(jnp.bfloat16)
                staged[i, q, levels:pad, :] = jnp.zeros((pad - levels, 128), jnp.bfloat16)

    def shift(k, s, action):
        at = (pl.ds(2 * k, 2), pl.ds(s * nq, nq))
        src, dst = staged.at[at], shifted.at[at]

        @pl.when(stays(k))
        def _():
            if action == "start":
                pltpu.make_async_copy(src, dst, shift_sems.at[1, k, s]).start()

        @pl.when(jnp.logical_not(stays(k)))
        def _():
            far = pltpu.make_async_remote_copy(
                src, dst, shift_sems.at[0, k, s], shift_sems.at[1, k, s],
                device_id={"lon": shift_to(k)[0], "lat": shift_to(k)[1]}, device_id_type=MESH,
            )
            if action == "start":
                far.start()
            else:
                far.wait_send()

    def first(k, s, action):
        src = shifted.at[pl.ds(2 * k, 2), pl.ds(s * nq, nq)]
        dst = rows_ref.at[pl.ds(1, 2), pl.ds(4 * (swapped if k == 0 else o) + s * nq, nq)]
        here = recv_sems.at[0, 0, core * SPLIT + s]
        lon, lat = relay(k)
        mine = (lat == t) & (lon == o)

        @pl.when(mine)
        def _():
            if action == "start":
                pltpu.make_async_copy(src, dst, here).start()

        @pl.when(jnp.logical_not(mine))
        def _():
            far = pltpu.make_async_remote_copy(
                src, dst, first_sems.at[k, s], here,
                device_id={"lon": lon, "lat": lat}, device_id_type=MESH,
            )
            if action == "start":
                far.start()
            else:
                far.wait_send()

    edge = (o == 0).astype(jnp.int32) + (o == 15).astype(jnp.int32)
    x_loads[0].wait()
    stage(0)
    pl.semaphore_wait(barrier, 25 - 2 * edge)
    parts = [(k, s) for s in range(SPLIT) for k in range(2)]
    for s in range(SPLIT):
        shift(0, s, "start")
    x_loads[1].wait()
    stage(1)
    for s in range(SPLIT):
        shift(1, s, "start")
    for load in weight_loads:
        load.start()

    for k, s in parts:
        dst = shifted.at[pl.ds(2 * k, 2), pl.ds(s * nq, nq)]
        pltpu.make_async_copy(dst, dst, shift_sems.at[1, k, s]).wait()
        first(k, s, "start")

    @pl.when(edge > 0)
    def _():
        row = jnp.where(o == 0, 0, 3)

        def fill(q, carry):
            rows_ref[row, q] = jnp.zeros((pad, 128), jnp.bfloat16)
            return carry

        lax.fori_loop(0, 64, fill, 0)

    band = jnp.int32(0)
    for b in range(8):
        band = jnp.where(slots_ref[b] == t, b, band)
    w0, w1, w2 = weights_ref[0, band], weights_ref[1, band], weights_ref[2, band]
    for load in weight_loads:
        load.wait()
    taps[...] = jnp.zeros_like(taps)
    for tap in range(-3, 4):
        total = jnp.zeros((128, 128), jnp.float32)
        for k in range(5):
            hit = (offsets_ref[band, k] == tap).astype(jnp.float32)
            total = total + hit * filters_ref[band, k].astype(jnp.float32)
        block = total.astype(jnp.bfloat16)
        for m in range(2):
            at = tap + 3 + m
            taps[at * 128 : (at + 1) * 128, m * 128 : (m + 1) * 128] = block
    chosen = lax.broadcasted_iota(jnp.int32, (levels, 8, levels), 1) == band
    picked = jnp.sum(jnp.where(chosen, vertical_ref[...].astype(jnp.float32), 0.0), axis=1)
    vert[...] = jnp.zeros_like(vert)
    vert[0:levels, 0:levels] = picked.astype(jnp.bfloat16)

    tables = [
        pltpu.make_async_copy(taps, taps_hbm, table_sems.at[0]),
        pltpu.make_async_copy(vert, vert_hbm, table_sems.at[1]),
    ]
    for table in tables:
        table.start()

    sends = []

    def block_of(dx, dz, j):
        return ((xh + dx) % 2) * 8 + ((z + dz + 8 - y - 2 * j) % 4) * 2 + j

    def rows_of(dx, dz, n):
        return pl.ds(block_of(dx, dz, n // SPLIT) * 4 + (n % SPLIT) * nq, nq)

    def piece(dx, dz, n):
        return rows_ref.at[pl.ds(1, 2), rows_of(dx, dz, n)]

    def send(dx, dz, n, to, there):
        ref = piece(dx, dz, n)
        copy = pltpu.make_async_remote_copy(
            ref, ref, send_sems.at[len(sends)], recv_sems.at[there[0], there[1], n],
            device_id={"lon": o, "lat": to}, device_id_type=MESH,
        )
        copy.start()
        sends.append(copy)

    def halo(dx, dz, n, side, partner=False):
        q = rows_of(dx, dz, n)
        src = rows_ref.at[1 + side, q]
        dst = rows_ref.at[3 - 3 * side, q]
        slot = block_of(dx, dz, n // SPLIT) * SPLIT + n % SPLIT
        own = block_of(dx + 1, dz, n // SPLIT) * SPLIT + n % SPLIT if partner else slot
        return pltpu.make_async_remote_copy(
            src, dst, halo_send.at[side, own], halo_recv.at[side, slot],
            device_id={"lon": o - 1 + 2 * side, "lat": xp if partner else t}, device_id_type=MESH,
        )

    def start_halo(dx, dz, n, side):
        if dx == 0:
            halo(dx, dz, n, side).start()

            @pl.when(crosses(side))
            def _():
                halo(dx, dz, n, side, True).start()
        else:
            @pl.when(jnp.logical_not(crosses(side)))
            def _():
                halo(dx, dz, n, side).start()

    def arrive(dx, dz, n):
        if (dx, dz) != (0, 0):
            ref = piece(dx, dz, n)
            pltpu.make_async_copy(ref, ref, recv_sems.at[dx, dz, n]).wait()
        late = n in LATE
        ring = dx == 0 or not late
        if dx == 0 and dz == 0:
            send(dx, dz, n, xp, (1, 0))
        if ring and dz == 0:
            send(dx, dz, n, zp, (dx, 3))
            send(dx, dz, n, zm, (dx, 1))
        if ring and dz == 3 and n < per // 2:
            send(dx, dz, n, zp, (dx, 2))
        if ring and dz == 1 and n >= per // 2:
            send(dx, dz, n, zm, (dx, 2))
        if dx == 0 and dz != 0 and late:
            send(dx, dz, n, xp, (1, dz))
        each_side(lambda side: start_halo(dx, dz, n, side))

    def blend_block(block):
        for s in range(SPLIT):
            for side, present in ((1, o > 0), (0, o < 15)):

                @pl.when(present)
                def _():
                    dst = rows_ref.at[3 - 3 * side, pl.ds(block * 4 + s * nq, nq)]
                    pltpu.make_async_copy(dst, dst, halo_recv.at[side, block * SPLIT + s]).wait()

        for q in range(4):
            rows = [rows_ref[i, block * 4 + q].astype(jnp.float32) for i in range(4)]
            m = (2 * block + (q + 1) // 2) % 32
            for i in range(2):
                value = w0 * rows[i] + w1 * rows[i + 1] + w2 * rows[i + 2]
                blended[i, m, 1 - q % 2] = value.astype(jnp.bfloat16)

    def keep(n, count, first):
        part = pl.ds(0, 2), pl.ds(first, count)
        return pltpu.make_async_copy(blended.at[part], blended_hbm.at[part], out_sems.at[n])

    def blend_own(n, carry):
        block = xh * 8 + n
        blend_block(block)

        @pl.when(n == 0)
        def _():
            keep(n, 1, 2 * block + 1).start()

        @pl.when(n > 0)
        def _():
            keep(n, 2, 2 * block).start()

        return carry

    def blend_other(n, carry):
        block = (1 - xh) * 8 + n
        blend_block(block)
        keep(8 + n, 2, 2 * block).start()
        return carry

    def inner_outputs():
        def body(n, carry):
            chunk_output(4 * xh + 1 + n, n, taps, vert, mixed, lambda i, m: load_pair(i, m % 32), done)
            pltpu.make_async_copy(done.at[n], inner_hbm.at[n], store_sems.at[n]).start()
            return carry

        lax.fori_loop(0, 2, body, 0)

    def load_pair(i, m):
        return jnp.concatenate([blended[i, m, 0], blended[i, m, 1]], axis=1)

    for n in range(per):
        ref = piece(0, 0, n)
        pltpu.make_async_copy(ref, ref, recv_sems.at[0, 0, n]).wait()
    for lon, lat in peers:
        pl.semaphore_signal(ready_sem, inc=1, device_id={"lon": lon, "lat": lat}, device_id_type=MESH)
    pl.semaphore_wait(ready_sem, 10)

    everything = range(per)
    late = [n for n in everything if n in LATE]
    early = [n for n in everything if n not in late]
    for dx, dz, which in ORDER_1:
        for n in {"all": everything, "late": late, "early": early}[which]:
            arrive(dx, dz, n)
    lax.fori_loop(0, 8, blend_own, 0)
    for dx, dz, which in ORDER_2:
        for n in {"all": everything, "late": late, "early": early}[which]:
            arrive(dx, dz, n)
    inner_outputs()
    lax.fori_loop(0, 8, blend_other, 0)
    keep(16, 1, 16 * xh).start()

    for table in tables:
        table.wait()
    for n in range(2):
        pltpu.make_async_copy(done.at[n], inner_hbm.at[n], store_sems.at[n]).wait()
    for n in range(17):
        keep(n, 1 if n in (0, 16) else 2, 0).wait()
    for k, s in parts:
        shift(k, s, "wait")
        first(k, s, "wait")
    for copy in sends:
        copy.wait_send()
    for dx in range(2):
        for dz in range(4):
            for n in range(per):
                each_side(lambda side: halo(dx, dz, n, side).wait_send())


ORDER_1 = [(0, 0, "all"), (0, 1, "all"), (0, 3, "all"), (1, 0, "all"), (0, 2, "all"), (1, 1, "early"), (1, 3, "early")]
ORDER_2 = [(1, 2, "early"), (1, 1, "late"), (1, 3, "late"), (1, 2, "late")]


def fused(weights, offsets, slots, x, filters, vertical, levels, pad):
    per = 2 * SPLIT
    smem, anywhere = pl.BlockSpec(memory_space=pltpu.SMEM), pl.BlockSpec(memory_space=pl.ANY)
    return pl.pallas_call(
        functools.partial(fused_kernel, levels, pad),
        out_shape=[
            jax.ShapeDtypeStruct((2, 32, 2, pad, 128), jnp.bfloat16),
            jax.ShapeDtypeStruct((2, 2, levels, 8, 128), jnp.bfloat16),
            jax.ShapeDtypeStruct((1024, 256), jnp.bfloat16),
            jax.ShapeDtypeStruct((pad, pad), jnp.bfloat16),
        ],
        in_specs=[smem, smem, smem, anywhere, anywhere, anywhere],
        out_specs=[anywhere] * 4,
        scratch_shapes=[
            pltpu.VMEM((16 * levels, 128), jnp.float32),
            pltpu.VMEM((8, 5, 128, 128), jnp.bfloat16),
            pltpu.VMEM((levels, 8, levels), jnp.bfloat16),
            pltpu.VMEM((4, 4, pad, 128), jnp.bfloat16),
            pltpu.VMEM((4, 4, pad, 128), jnp.bfloat16),
            pltpu.VMEM((4, 64, pad, 128), jnp.bfloat16),
            pltpu.VMEM((2, 32, 2, pad, 128), jnp.bfloat16),
            pltpu.VMEM((1024, 256), jnp.bfloat16),
            pltpu.VMEM((pad, pad), jnp.bfloat16),
            pltpu.VMEM((2, pad * 8, 128), jnp.float32),
            pltpu.VMEM((2, 2, levels, 8, 128), jnp.bfloat16),
            pltpu.SemaphoreType.DMA((4,)),
            pltpu.SemaphoreType.DMA((32 * SPLIT,)),
            pltpu.SemaphoreType.DMA((2, 2, SPLIT)),
            pltpu.SemaphoreType.DMA((2, SPLIT)),
            pltpu.SemaphoreType.DMA((2, 4, per)),
            pltpu.SemaphoreType.DMA((2, 8 * per)),
            pltpu.SemaphoreType.DMA((2, 8 * per)),
            pltpu.SemaphoreType.REGULAR,
            pltpu.SemaphoreType.DMA((2,)),
            pltpu.SemaphoreType.DMA((17,)),
            pltpu.SemaphoreType.DMA((2,)),
        ],
        compiler_params=pltpu.CompilerParams(
            collective_id=0, has_side_effects=True, vmem_limit_bytes=VMEM_MIB << 20
        ),
        name="fused",
    )(weights, offsets, slots, x, filters, vertical)


VMEM_MIB = 60
OUTER_MIB = 60


def on_device(grad_field, lat_weights, block_offsets, filters, vertical, slot_of_band):
    levels = grad_field.shape[2]
    pad = (levels + 15) // 16 * 16
    x = grad_field.transpose(0, 2, 1, 3).reshape(-1, 128)
    blended, inner, taps, vert = fused(
        lat_weights.T, block_offsets, slot_of_band, x, filters, vertical.transpose(1, 0, 2), levels, pad
    )
    out = outer_outputs(blended, inner, taps, vert, levels, pad)
    return out.transpose(0, 1, 3, 2, 4)


def solution(mesh):
    placed = (P("lat", "lon", None, None), P(), P(), P(), P(), P())
    return jax.shard_map(
        on_device,
        mesh=mesh,
        in_specs=placed,
        out_specs=P("lat", "lon", None, None, None),
        check_vma=False,
    )
```

```python
import functools

import jax
import jax.numpy as jnp
from jax import lax
from jax.experimental import pallas as pl
from jax.experimental.pallas import tpu as pltpu
from jax.sharding import PartitionSpec as P

MESH = pl.DeviceIdType.MESH
SPLIT = 2
LATE = (3,)


def chunk_output(chunk, slot, taps, vert, mixed, load_pair, done):
    levels, pad = done.shape[-3], vert.shape[0]
    lhs = []
    for i in range(2):
        pairs = [load_pair(i, chunk * 4 + n + 31) for n in range(7)]
        lhs.append(jnp.concatenate([jnp.concatenate(pairs[k : k + 4], axis=0) for k in range(4)], axis=1))
    lhs = jnp.concatenate(lhs, axis=0)
    smooth = jnp.dot(lhs, taps[...], preferred_element_type=jnp.float32).astype(jnp.bfloat16)
    wide = jnp.concatenate([smooth[p * pad : (p + 1) * pad] for p in range(8)], axis=1)
    result = jnp.dot(vert[...], wide, preferred_element_type=jnp.float32)
    for i in range(2):
        for n in range(8):
            at = (8 * i + n) * 128
            mixed[i, pl.ds(n, pad, stride=8), :] = result[:, at : at + 128]
        flat = mixed[i, 0 : levels * 8, :].reshape(levels, 8, 128)
        done[slot, i] = flat.astype(jnp.bfloat16)


def outer_kernel(levels, blended_hbm, inner_hbm, taps_hbm, vert_hbm, out_hbm, blended, taps, vert, mixed, done, ready, load_sems, inner_sems, store_sems):
    xh = lax.axis_index("lat") // 4

    def group(k):
        part = pl.ds(0, 2), pl.ds(((4 * xh + 2 + k) % 8) * 4, 4)
        return pltpu.make_async_copy(blended_hbm.at[part], blended.at[part], load_sems.at[k])

    def place(chunk):
        return out_hbm.at[0, pl.ds(0, 2), pl.ds(0, levels), pl.ds(pl.multiple_of(chunk * 8, 8), 8)]

    def store(slot, chunk):
        return pltpu.make_async_copy(done.at[slot], place(chunk), store_sems.at[slot])

    tables = [
        pltpu.make_async_copy(taps_hbm, taps, load_sems.at[8]),
        pltpu.make_async_copy(vert_hbm, vert, load_sems.at[9]),
    ]
    loads = [pltpu.make_async_copy(inner_hbm.at[n], ready.at[n], inner_sems.at[n]) for n in range(2)]
    inner = [pltpu.make_async_copy(ready.at[n], place(4 * xh + 1 + n), inner_sems.at[2 + n]) for n in range(2)]
    for k in range(3):
        group(k).start()
    for copy in tables:
        copy.start()
    for k in range(3, 8):
        group(k).start()
    for copy in loads:
        copy.start()
    for k in range(2):
        group(k).wait()
    for copy in tables:
        copy.wait()

    def load_pair(i, m):
        return jnp.concatenate([blended[i, m % 32, 0], blended[i, m % 32, 1]], axis=1)

    def body(n, carry):
        group(n + 2).wait()
        chunk = (4 * xh + 3 + n) % 8

        @pl.when(n >= 2)
        def _():
            store(n % 2, chunk).wait()

        chunk_output(chunk, n % 2, taps, vert, mixed, load_pair, done)
        store(n % 2, chunk).start()

        @pl.when(n == 2)
        def _():
            for load, copy in zip(loads, inner):
                load.wait()
                copy.start()

        return carry

    lax.fori_loop(0, 6, body, 0)
    for slot in range(2):
        store(slot, 0).wait()
    for copy in inner:
        copy.wait()


def outer_outputs(blended, inner, taps, vert, levels, pad):
    anywhere = pl.BlockSpec(memory_space=pl.ANY)
    return pl.pallas_call(
        functools.partial(outer_kernel, levels),
        out_shape=jax.ShapeDtypeStruct((1, 2, levels, 64, 128), jnp.bfloat16),
        in_specs=[anywhere] * 4,
        out_specs=anywhere,
        scratch_shapes=[
            pltpu.VMEM((2, 32, 2, pad, 128), jnp.bfloat16),
            pltpu.VMEM((1024, 256), jnp.bfloat16),
            pltpu.VMEM((pad, pad), jnp.bfloat16),
            pltpu.VMEM((2, pad * 8, 128), jnp.float32),
            pltpu.VMEM((2, 2, levels, 8, 128), jnp.bfloat16),
            pltpu.VMEM((2, 2, levels, 8, 128), jnp.bfloat16),
            pltpu.SemaphoreType.DMA((10,)),
            pltpu.SemaphoreType.DMA((4,)),
            pltpu.SemaphoreType.DMA((2,)),
        ],
        compiler_params=pltpu.CompilerParams(vmem_limit_bytes=OUTER_MIB << 20),
        name="outer_outputs",
    )(blended, inner, taps, vert)


def fused_kernel(
    levels, pad,
    weights_ref, offsets_ref, slots_ref, x_hbm, filters_hbm, vertical_hbm,
    blended_hbm, inner_hbm, taps_hbm, vert_hbm,
    x_ref, filters_ref, vertical_ref, staged, shifted, rows_ref, blended, taps, vert, mixed, done,
    load_sems, send_sems, shift_sems, first_sems, recv_sems, halo_send, halo_recv, ready_sem, shifted_sem, store_sems, out_sems, table_sems,
):
    o, t = lax.axis_index("lon"), lax.axis_index("lat")
    xh, z = t // 4, t % 4
    xl, y, core = o // 8, (o // 2) % 4, o % 2
    x = 2 * xh + xl
    zp, zm = xh * 4 + (z + 1) % 4, xh * 4 + (z + 3) % 4
    xp = (1 - xh) * 4 + z
    nq = 4 // SPLIT
    per = 2 * SPLIT
    half = 2 * levels * 4

    x_loads = [
        pltpu.make_async_copy(x_hbm.at[pl.ds(k * half, half)], x_ref.at[pl.ds(k * half, half)], load_sems.at[k])
        for k in range(2)
    ]
    weight_loads = [
        pltpu.make_async_copy(filters_hbm, filters_ref, load_sems.at[2]),
        pltpu.make_async_copy(vertical_hbm, vertical_ref, load_sems.at[3]),
    ]
    for load in x_loads:
        load.start()

    ahead = (y + 2 * core) % 4
    row_group = (z + 8 - y - 2 * core) % 4
    swapped = xh * 8 + y * 2 + core

    def shift_to(k):
        return (swapped, xl * 4 + (z + ahead) % 4) if k == 0 else (o, xh * 4 + (z + ahead) % 4)

    def shift_from(k):
        return (swapped, xl * 4 + (z + 4 - ahead) % 4) if k == 0 else (o, xh * 4 + (z + 4 - ahead) % 4)

    def stays(k):
        return (ahead == 0) & (xh == xl) if k == 0 else ahead == 0

    def relay(k):
        return (xl * 8 + row_group * 2, t) if k == 0 else (xh * 8 + row_group * 2 + 1, xl * 4 + z)

    def source(j):
        place = ((z + 8 - y - 2 * j) % 4) * 2 + j
        return jnp.where(core == 0, xl, xh) * 8 + place, jnp.where(core == 0, t, xl * 4 + z)

    barrier = pltpu.get_barrier_semaphore()

    def greet(lon, lat):
        pl.semaphore_signal(barrier, inc=1, device_id={"lon": lon, "lat": lat}, device_id_type=MESH)

    for k in range(2):
        greet(*shift_to(k))
        greet(*shift_from(k))
        greet(*relay(k))
        greet(*source(k))
    for lat in (zp, zm, xp):
        greet(o, lat)
    peers = [(o, xh * 4 + (z + n) % 4) for n in (1, 2, 3)]
    peers += [(((x + n) % 2) * 8 + y * 2 + core, ((x + n) % 4) // 2 * 4 + z) for n in (1, 2, 3)]
    for lon, lat in peers:
        greet(lon, lat)

    def each_side(action):
        @pl.when(o > 0)
        def _():
            action(0)

        @pl.when(o < 15)
        def _():
            action(1)

    def crosses(side):
        return o == (8 if side == 0 else 7)

    def greet_side(side):
        greet(o - 1 + 2 * side, t)
        greet(o - 1 + 2 * side, jnp.where(crosses(side), xp, t))

    each_side(greet_side)

    def stage(k):
        for i in (2 * k, 2 * k + 1):
            for q in range(4):
                value = x_ref[pl.ds(i * levels * 4 + q, levels, stride=4), :]
                staged[i, q, 0:levels, :] = value.astype(jnp.bfloat16)
                staged[i, q, levels:pad, :] = jnp.zeros((pad - levels, 128), jnp.bfloat16)

    def shift(k, s, action):
        at = (pl.ds(2 * k, 2), pl.ds(s * nq, nq))
        src, dst = staged.at[at], shifted.at[at]

        @pl.when(stays(k))
        def _():
            if action == "start":
                pltpu.make_async_copy(src, dst, shift_sems.at[1, k, s]).start()

        @pl.when(jnp.logical_not(stays(k)))
        def _():
            far = pltpu.make_async_remote_copy(
                src, dst, shift_sems.at[0, k, s], shift_sems.at[1, k, s],
                device_id={"lon": shift_to(k)[0], "lat": shift_to(k)[1]}, device_id_type=MESH,
            )
            if action == "start":
                far.start()
            else:
                far.wait_send()

    def first(k, s, action):
        src = shifted.at[pl.ds(2 * k, 2), pl.ds(s * nq, nq)]
        dst = rows_ref.at[pl.ds(1, 2), pl.ds(4 * (swapped if k == 0 else o) + s * nq, nq)]
        here = recv_sems.at[0, 0, core * SPLIT + s]
        lon, lat = relay(k)
        mine = (lat == t) & (lon == o)

        @pl.when(mine)
        def _():
            if action == "start":
                pltpu.make_async_copy(src, dst, here).start()

        @pl.when(jnp.logical_not(mine))
        def _():
            far = pltpu.make_async_remote_copy(
                src, dst, first_sems.at[k, s], here,
                device_id={"lon": lon, "lat": lat}, device_id_type=MESH,
            )
            if action == "start":
                far.start()
            else:
                far.wait_send()

    edge = (o == 0).astype(jnp.int32) + (o == 15).astype(jnp.int32)
    x_loads[0].wait()
    stage(0)
    pl.semaphore_wait(barrier, 21 - 2 * edge)
    parts = [(k, s) for s in range(SPLIT) for k in range(2)]
    for s in range(SPLIT):
        shift(0, s, "start")
    x_loads[1].wait()
    stage(1)
    for s in range(SPLIT):
        shift(1, s, "start")
    for load in weight_loads:
        load.start()

    for k, s in parts:
        dst = shifted.at[pl.ds(2 * k, 2), pl.ds(s * nq, nq)]
        pltpu.make_async_copy(dst, dst, shift_sems.at[1, k, s]).wait()
        first(k, s, "start")

    for lon, lat in peers[:3]:
        pl.semaphore_signal(shifted_sem, inc=1, device_id={"lon": lon, "lat": lat}, device_id_type=MESH)

    @pl.when(edge > 0)
    def _():
        row = jnp.where(o == 0, 0, 3)

        def fill(q, carry):
            rows_ref[row, q] = jnp.zeros((pad, 128), jnp.bfloat16)
            return carry

        lax.fori_loop(0, 64, fill, 0)

    band = jnp.int32(0)
    for b in range(8):
        band = jnp.where(slots_ref[b] == t, b, band)
    w0, w1, w2 = weights_ref[0, band], weights_ref[1, band], weights_ref[2, band]
    for load in weight_loads:
        load.wait()
    taps[...] = jnp.zeros_like(taps)
    for tap in range(-3, 4):
        total = jnp.zeros((128, 128), jnp.float32)
        for k in range(5):
            hit = (offsets_ref[band, k] == tap).astype(jnp.float32)
            total = total + hit * filters_ref[band, k].astype(jnp.float32)
        block = total.astype(jnp.bfloat16)
        for m in range(2):
            at = tap + 3 + m
            taps[at * 128 : (at + 1) * 128, m * 128 : (m + 1) * 128] = block
    chosen = lax.broadcasted_iota(jnp.int32, (levels, 8, levels), 1) == band
    picked = jnp.sum(jnp.where(chosen, vertical_ref[...].astype(jnp.float32), 0.0), axis=1)
    vert[...] = jnp.zeros_like(vert)
    vert[0:levels, 0:levels] = picked.astype(jnp.bfloat16)

    tables = [
        pltpu.make_async_copy(taps, taps_hbm, table_sems.at[0]),
        pltpu.make_async_copy(vert, vert_hbm, table_sems.at[1]),
    ]
    for table in tables:
        table.start()

    sends = []

    def block_of(dx, dz, j):
        return ((xh + dx) % 2) * 8 + ((z + dz + 8 - y - 2 * j) % 4) * 2 + j

    def rows_of(dx, dz, n):
        return pl.ds(block_of(dx, dz, n // SPLIT) * 4 + (n % SPLIT) * nq, nq)

    def piece(dx, dz, n):
        return rows_ref.at[pl.ds(1, 2), rows_of(dx, dz, n)]

    def send(dx, dz, n, to, there, only=None):
        ref = piece(dx, dz, n)
        copy = pltpu.make_async_remote_copy(
            ref, ref, send_sems.at[len(sends)], recv_sems.at[there[0], there[1], n],
            device_id={"lon": o, "lat": to}, device_id_type=MESH,
        )
        sends.append((copy, only))
        if only is None:
            copy.start()
        else:
            pl.when(only)(copy.start)

    def halo(dx, dz, n, side, partner=False):
        q = rows_of(dx, dz, n)
        src = rows_ref.at[1 + side, q]
        dst = rows_ref.at[3 - 3 * side, q]
        slot = block_of(dx, dz, n // SPLIT) * SPLIT + n % SPLIT
        own = block_of(dx + 1, dz, n // SPLIT) * SPLIT + n % SPLIT if partner else slot
        return pltpu.make_async_remote_copy(
            src, dst, halo_send.at[side, own], halo_recv.at[side, slot],
            device_id={"lon": o - 1 + 2 * side, "lat": xp if partner else t}, device_id_type=MESH,
        )

    def start_halo(dx, dz, n, side):
        if dx == 0:
            halo(dx, dz, n, side).start()

            @pl.when(crosses(side))
            def _():
                halo(dx, dz, n, side, True).start()
        else:
            @pl.when(jnp.logical_not(crosses(side)))
            def _():
                halo(dx, dz, n, side).start()

    boundary = ((xl == 0) & (y == 3)) | ((xl == 1) & (y == 0))

    def ring_start(dx, n, only=None):
        send(dx, 0, n, zp, (dx, 3), only)
        send(dx, 0, n, zm, (dx, 1), only)

    def arrive(dx, dz, n):
        if (dx, dz) != (0, 0):
            ref = piece(dx, dz, n)
            pltpu.make_async_copy(ref, ref, recv_sems.at[dx, dz, n]).wait()
        late = n in LATE
        only = boundary if dx == 1 and late else None
        if (dx, dz) == (0, 0):
            send(dx, dz, n, xp, (1, 0))
        elif dz == 0:
            ring_start(dx, n, only)
        if dz == 3 and n < per // 2:
            send(dx, dz, n, zp, (dx, 2), only)
        if dz == 1 and n >= per // 2:
            send(dx, dz, n, zm, (dx, 2), only)
        if dx == 0 and dz != 0 and late:
            send(dx, dz, n, xp, (1, dz), jnp.logical_not(boundary))
        each_side(lambda side: start_halo(dx, dz, n, side))

    def blend_block(block):
        for s in range(SPLIT):
            for side, present in ((1, o > 0), (0, o < 15)):

                @pl.when(present)
                def _():
                    dst = rows_ref.at[3 - 3 * side, pl.ds(block * 4 + s * nq, nq)]
                    pltpu.make_async_copy(dst, dst, halo_recv.at[side, block * SPLIT + s]).wait()

        for q in range(4):
            rows = [rows_ref[i, block * 4 + q].astype(jnp.float32) for i in range(4)]
            m = (2 * block + (q + 1) // 2) % 32
            for i in range(2):
                value = w0 * rows[i] + w1 * rows[i + 1] + w2 * rows[i + 2]
                blended[i, m, 1 - q % 2] = value.astype(jnp.bfloat16)

    def keep(n, count, first):
        part = pl.ds(0, 2), pl.ds(first, count)
        return pltpu.make_async_copy(blended.at[part], blended_hbm.at[part], out_sems.at[n])

    def blend_own(n, carry):
        block = xh * 8 + n
        blend_block(block)

        @pl.when(n == 0)
        def _():
            keep(n, 1, 2 * block + 1).start()

        @pl.when(n > 0)
        def _():
            keep(n, 2, 2 * block).start()

        return carry

    def blend_other(n, carry):
        block = (1 - xh) * 8 + n
        blend_block(block)
        keep(8 + n, 2, 2 * block).start()
        return carry

    def inner_outputs():
        def body(n, carry):
            chunk_output(4 * xh + 1 + n, n, taps, vert, mixed, lambda i, m: load_pair(i, m % 32), done)
            pltpu.make_async_copy(done.at[n], inner_hbm.at[n], store_sems.at[n]).start()
            return carry

        lax.fori_loop(0, 2, body, 0)

    def load_pair(i, m):
        return jnp.concatenate([blended[i, m, 0], blended[i, m, 1]], axis=1)

    for n in range(per):
        ref = piece(0, 0, n)
        pltpu.make_async_copy(ref, ref, recv_sems.at[0, 0, n]).wait()
        if n == 0:
            pl.semaphore_wait(shifted_sem, 3)
        ring_start(0, n)
    for lon, lat in peers:
        pl.semaphore_signal(ready_sem, inc=1, device_id={"lon": lon, "lat": lat}, device_id_type=MESH)
    pl.semaphore_wait(ready_sem, NPEERS)

    everything = range(per)
    late = [n for n in everything if n in LATE]
    early = [n for n in everything if n not in late]
    for dx, dz, which in ORDER_1:
        for n in {"all": everything, "late": late, "early": early}[which]:
            arrive(dx, dz, n)
    lax.fori_loop(0, 8, blend_own, 0)
    for dx, dz, which in ORDER_2:
        for n in {"all": everything, "late": late, "early": early}[which]:
            arrive(dx, dz, n)
    inner_outputs()
    lax.fori_loop(0, 8, blend_other, 0)
    keep(16, 1, 16 * xh).start()

    for table in tables:
        table.wait()
    for n in range(2):
        pltpu.make_async_copy(done.at[n], inner_hbm.at[n], store_sems.at[n]).wait()
    for n in range(17):
        keep(n, 1 if n in (0, 16) else 2, 0).wait()
    for k, s in parts:
        shift(k, s, "wait")
        first(k, s, "wait")
    for copy, only in sends:
        if only is None:
            copy.wait_send()
        else:
            pl.when(only)(copy.wait_send)
    for dx in range(2):
        for dz in range(4):
            for n in range(per):
                each_side(lambda side: halo(dx, dz, n, side).wait_send())


ORDER_1 = [(0, 0, "all"), (0, 1, "all"), (0, 3, "all"), (1, 0, "all"), (0, 2, "all"), (1, 1, "all"), (1, 3, "all")]
ORDER_2 = [(1, 2, "all")]


def fused(weights, offsets, slots, x, filters, vertical, levels, pad):
    per = 2 * SPLIT
    smem, anywhere = pl.BlockSpec(memory_space=pltpu.SMEM), pl.BlockSpec(memory_space=pl.ANY)
    return pl.pallas_call(
        functools.partial(fused_kernel, levels, pad),
        out_shape=[
            jax.ShapeDtypeStruct((2, 32, 2, pad, 128), jnp.bfloat16),
            jax.ShapeDtypeStruct((2, 2, levels, 8, 128), jnp.bfloat16),
            jax.ShapeDtypeStruct((1024, 256), jnp.bfloat16),
            jax.ShapeDtypeStruct((pad, pad), jnp.bfloat16),
        ],
        in_specs=[smem, smem, smem, anywhere, anywhere, anywhere],
        out_specs=[anywhere] * 4,
        scratch_shapes=[
            pltpu.VMEM((16 * levels, 128), jnp.float32),
            pltpu.VMEM((8, 5, 128, 128), jnp.bfloat16),
            pltpu.VMEM((levels, 8, levels), jnp.bfloat16),
            pltpu.VMEM((4, 4, pad, 128), jnp.bfloat16),
            pltpu.VMEM((4, 4, pad, 128), jnp.bfloat16),
            pltpu.VMEM((4, 64, pad, 128), jnp.bfloat16),
            pltpu.VMEM((2, 32, 2, pad, 128), jnp.bfloat16),
            pltpu.VMEM((1024, 256), jnp.bfloat16),
            pltpu.VMEM((pad, pad), jnp.bfloat16),
            pltpu.VMEM((2, pad * 8, 128), jnp.float32),
            pltpu.VMEM((2, 2, levels, 8, 128), jnp.bfloat16),
            pltpu.SemaphoreType.DMA((4,)),
            pltpu.SemaphoreType.DMA((48 * SPLIT,)),
            pltpu.SemaphoreType.DMA((2, 2, SPLIT)),
            pltpu.SemaphoreType.DMA((2, SPLIT)),
            pltpu.SemaphoreType.DMA((2, 4, per)),
            pltpu.SemaphoreType.DMA((2, 8 * per)),
            pltpu.SemaphoreType.DMA((2, 8 * per)),
            pltpu.SemaphoreType.REGULAR,
            pltpu.SemaphoreType.REGULAR,
            pltpu.SemaphoreType.DMA((2,)),
            pltpu.SemaphoreType.DMA((17,)),
            pltpu.SemaphoreType.DMA((2,)),
        ],
        compiler_params=pltpu.CompilerParams(
            collective_id=0, has_side_effects=True, vmem_limit_bytes=VMEM_MIB << 20
        ),
        name="fused",
    )(weights, offsets, slots, x, filters, vertical)


NPEERS = 6
VMEM_MIB = 60
OUTER_MIB = 60


def on_device(grad_field, lat_weights, block_offsets, filters, vertical, slot_of_band):
    levels = grad_field.shape[2]
    pad = (levels + 15) // 16 * 16
    x = grad_field.transpose(0, 2, 1, 3).reshape(-1, 128)
    blended, inner, taps, vert = fused(
        lat_weights.T, block_offsets, slot_of_band, x, filters, vertical.transpose(1, 0, 2), levels, pad
    )
    out = outer_outputs(blended, inner, taps, vert, levels, pad)
    return out.transpose(0, 1, 3, 2, 4)


def solution(mesh):
    placed = (P("lat", "lon", None, None), P(), P(), P(), P(), P())
    return jax.shard_map(
        on_device,
        mesh=mesh,
        in_specs=placed,
        out_specs=P("lat", "lon", None, None, None),
        check_vma=False,
    )
```

```python
import functools

import jax
import jax.numpy as jnp
from jax import lax
from jax.experimental import pallas as pl
from jax.experimental.pallas import tpu as pltpu
from jax.sharding import PartitionSpec as P

MESH = pl.DeviceIdType.MESH
SPLIT = 2
LATE = (3,)


def chunk_output(chunk, slot, taps, vert, mixed, load_pair, done):
    levels, pad = done.shape[-3], vert.shape[0]
    lhs = []
    for i in range(2):
        pairs = [load_pair(i, chunk * 4 + n + 31) for n in range(7)]
        lhs.append(jnp.concatenate([jnp.concatenate(pairs[k : k + 4], axis=0) for k in range(4)], axis=1))
    lhs = jnp.concatenate(lhs, axis=0)
    smooth = jnp.dot(lhs, taps[...], preferred_element_type=jnp.float32).astype(jnp.bfloat16)
    wide = jnp.concatenate([smooth[p * pad : (p + 1) * pad] for p in range(8)], axis=1)
    result = jnp.dot(vert[...], wide, preferred_element_type=jnp.float32)
    for i in range(2):
        for n in range(8):
            at = (8 * i + n) * 128
            mixed[i, pl.ds(n, pad, stride=8), :] = result[:, at : at + 128]
        flat = mixed[i, 0 : levels * 8, :].reshape(levels, 8, 128)
        done[slot, i] = flat.astype(jnp.bfloat16)


def outer_kernel(levels, blended_hbm, inner_hbm, taps_hbm, vert_hbm, out_hbm, blended, taps, vert, mixed, done, ready, load_sems, inner_sems, store_sems):
    xh = lax.axis_index("lat") // 4

    def group(k):
        part = pl.ds(0, 2), pl.ds(((4 * xh + 2 + k) % 8) * 4, 4)
        return pltpu.make_async_copy(blended_hbm.at[part], blended.at[part], load_sems.at[k])

    def place(chunk):
        return out_hbm.at[0, pl.ds(0, 2), pl.ds(0, levels), pl.ds(pl.multiple_of(chunk * 8, 8), 8)]

    def store(slot, chunk):
        return pltpu.make_async_copy(done.at[slot], place(chunk), store_sems.at[slot])

    tables = [
        pltpu.make_async_copy(taps_hbm, taps, load_sems.at[8]),
        pltpu.make_async_copy(vert_hbm, vert, load_sems.at[9]),
    ]
    loads = [pltpu.make_async_copy(inner_hbm.at[n], ready.at[n], inner_sems.at[n]) for n in range(2)]
    inner = [pltpu.make_async_copy(ready.at[n], place(4 * xh + 1 + n), inner_sems.at[2 + n]) for n in range(2)]
    for k in range(3):
        group(k).start()
    for copy in tables:
        copy.start()
    for k in range(3, 8):
        group(k).start()
    for copy in loads:
        copy.start()
    for k in range(2):
        group(k).wait()
    for copy in tables:
        copy.wait()

    def load_pair(i, m):
        return jnp.concatenate([blended[i, m % 32, 0], blended[i, m % 32, 1]], axis=1)

    def body(n, carry):
        group(n + 2).wait()
        chunk = (4 * xh + 3 + n) % 8

        @pl.when(n >= 2)
        def _():
            store(n % 2, chunk).wait()

        chunk_output(chunk, n % 2, taps, vert, mixed, load_pair, done)
        store(n % 2, chunk).start()

        @pl.when(n == 2)
        def _():
            for load, copy in zip(loads, inner):
                load.wait()
                copy.start()

        return carry

    lax.fori_loop(0, 6, body, 0)
    for slot in range(2):
        store(slot, 0).wait()
    for copy in inner:
        copy.wait()


def outer_outputs(blended, inner, taps, vert, levels, pad):
    anywhere = pl.BlockSpec(memory_space=pl.ANY)
    return pl.pallas_call(
        functools.partial(outer_kernel, levels),
        out_shape=jax.ShapeDtypeStruct((1, 2, levels, 64, 128), jnp.bfloat16),
        in_specs=[anywhere] * 4,
        out_specs=anywhere,
        scratch_shapes=[
            pltpu.VMEM((2, 32, 2, pad, 128), jnp.bfloat16),
            pltpu.VMEM((1024, 256), jnp.bfloat16),
            pltpu.VMEM((pad, pad), jnp.bfloat16),
            pltpu.VMEM((2, pad * 8, 128), jnp.float32),
            pltpu.VMEM((2, 2, levels, 8, 128), jnp.bfloat16),
            pltpu.VMEM((2, 2, levels, 8, 128), jnp.bfloat16),
            pltpu.SemaphoreType.DMA((10,)),
            pltpu.SemaphoreType.DMA((4,)),
            pltpu.SemaphoreType.DMA((2,)),
        ],
        compiler_params=pltpu.CompilerParams(vmem_limit_bytes=OUTER_MIB << 20),
        name="outer_outputs",
    )(blended, inner, taps, vert)


def fused_kernel(
    levels, pad,
    weights_ref, offsets_ref, slots_ref, x_hbm, filters_hbm, vertical_hbm,
    blended_hbm, inner_hbm, taps_hbm, vert_hbm,
    x_ref, filters_ref, vertical_ref, staged, shifted, rows_ref, blended, taps, vert, mixed, done,
    load_sems, send_sems, shift_sems, first_sems, recv_sems, halo_send, halo_recv, ready_sem, shifted_sem, store_sems, out_sems, table_sems,
):
    o, t = lax.axis_index("lon"), lax.axis_index("lat")
    xh, z = t // 4, t % 4
    xl, y, core = o // 8, (o // 2) % 4, o % 2
    x = 2 * xh + xl
    zp, zm = xh * 4 + (z + 1) % 4, xh * 4 + (z + 3) % 4
    xp = (1 - xh) * 4 + z
    nq = 4 // SPLIT
    per = 2 * SPLIT
    half = 2 * levels * 4

    x_loads = [
        pltpu.make_async_copy(x_hbm.at[pl.ds(k * half, half)], x_ref.at[pl.ds(k * half, half)], load_sems.at[k])
        for k in range(2)
    ]
    weight_loads = [
        pltpu.make_async_copy(filters_hbm, filters_ref, load_sems.at[2]),
        pltpu.make_async_copy(vertical_hbm, vertical_ref, load_sems.at[3]),
    ]
    for load in x_loads:
        load.start()

    ahead = (y + 2 * core) % 4
    row_group = (z + 8 - y - 2 * core) % 4
    swapped = xh * 8 + y * 2 + core

    def shift_to(k):
        return (swapped, xl * 4 + (z + ahead) % 4) if k == 0 else (o, xh * 4 + (z + ahead) % 4)

    def shift_from(k):
        return (swapped, xl * 4 + (z + 4 - ahead) % 4) if k == 0 else (o, xh * 4 + (z + 4 - ahead) % 4)

    def stays(k):
        return (ahead == 0) & (xh == xl) if k == 0 else ahead == 0

    def relay(k):
        return (xl * 8 + row_group * 2, t) if k == 0 else (xh * 8 + row_group * 2 + 1, xl * 4 + z)

    def source(j):
        place = ((z + 8 - y - 2 * j) % 4) * 2 + j
        return jnp.where(core == 0, xl, xh) * 8 + place, jnp.where(core == 0, t, xl * 4 + z)

    barrier = pltpu.get_barrier_semaphore()

    def greet(lon, lat):
        pl.semaphore_signal(barrier, inc=1, device_id={"lon": lon, "lat": lat}, device_id_type=MESH)

    for k in range(2):
        greet(*shift_to(k))
        greet(*shift_from(k))
        greet(*relay(k))
        greet(*source(k))
    for lat in (zp, zm, xp):
        greet(o, lat)
    peers = [(o, xh * 4 + (z + n) % 4) for n in (1, 2, 3)]
    peers += [(((x + n) % 2) * 8 + y * 2 + core, ((x + n) % 4) // 2 * 4 + z) for n in (1, 2, 3)]
    for lon, lat in peers:
        greet(lon, lat)

    def each_side(action):
        @pl.when(o > 0)
        def _():
            action(0)

        @pl.when(o < 15)
        def _():
            action(1)

    def crosses(side):
        return o == (8 if side == 0 else 7)

    def greet_side(side):
        greet(o - 1 + 2 * side, t)
        greet(o - 1 + 2 * side, jnp.where(crosses(side), xp, t))

    each_side(greet_side)

    def stage(k):
        for i in (2 * k, 2 * k + 1):
            for q in range(4):
                value = x_ref[pl.ds(i * levels * 4 + q, levels, stride=4), :]
                staged[i, q, 0:levels, :] = value.astype(jnp.bfloat16)
                staged[i, q, levels:pad, :] = jnp.zeros((pad - levels, 128), jnp.bfloat16)

    def shift(k, s, action):
        at = (pl.ds(2 * k, 2), pl.ds(s * nq, nq))
        src, dst = staged.at[at], shifted.at[at]

        @pl.when(stays(k))
        def _():
            if action == "start":
                pltpu.make_async_copy(src, dst, shift_sems.at[1, k, s]).start()

        @pl.when(jnp.logical_not(stays(k)))
        def _():
            far = pltpu.make_async_remote_copy(
                src, dst, shift_sems.at[0, k, s], shift_sems.at[1, k, s],
                device_id={"lon": shift_to(k)[0], "lat": shift_to(k)[1]}, device_id_type=MESH,
            )
            if action == "start":
                far.start()
            else:
                far.wait_send()

    def first(k, s, action):
        src = shifted.at[pl.ds(2 * k, 2), pl.ds(s * nq, nq)]
        dst = rows_ref.at[pl.ds(1, 2), pl.ds(4 * (swapped if k == 0 else o) + s * nq, nq)]
        here = recv_sems.at[0, 0, core * SPLIT + s]
        lon, lat = relay(k)
        mine = (lat == t) & (lon == o)

        @pl.when(mine)
        def _():
            if action == "start":
                pltpu.make_async_copy(src, dst, here).start()

        @pl.when(jnp.logical_not(mine))
        def _():
            far = pltpu.make_async_remote_copy(
                src, dst, first_sems.at[k, s], here,
                device_id={"lon": lon, "lat": lat}, device_id_type=MESH,
            )
            if action == "start":
                far.start()
            else:
                far.wait_send()

    edge = (o == 0).astype(jnp.int32) + (o == 15).astype(jnp.int32)
    x_loads[0].wait()
    stage(0)
    pl.semaphore_wait(barrier, 21 - 2 * edge)
    parts = [(k, s) for s in range(SPLIT) for k in range(2)]
    for s in range(SPLIT):
        shift(0, s, "start")
    x_loads[1].wait()
    stage(1)
    for s in range(SPLIT):
        shift(1, s, "start")
    for load in weight_loads:
        load.start()

    for k, s in parts:
        dst = shifted.at[pl.ds(2 * k, 2), pl.ds(s * nq, nq)]
        pltpu.make_async_copy(dst, dst, shift_sems.at[1, k, s]).wait()
        first(k, s, "start")

    for lon, lat in peers[:3]:
        pl.semaphore_signal(shifted_sem, inc=1, device_id={"lon": lon, "lat": lat}, device_id_type=MESH)

    @pl.when(edge > 0)
    def _():
        row = jnp.where(o == 0, 0, 3)

        def fill(q, carry):
            rows_ref[row, q] = jnp.zeros((pad, 128), jnp.bfloat16)
            return carry

        lax.fori_loop(0, 64, fill, 0)

    band = jnp.int32(0)
    for b in range(8):
        band = jnp.where(slots_ref[b] == t, b, band)
    w0, w1, w2 = weights_ref[0, band], weights_ref[1, band], weights_ref[2, band]
    for load in weight_loads:
        load.wait()
    taps[...] = jnp.zeros_like(taps)
    for tap in range(-3, 4):
        total = jnp.zeros((128, 128), jnp.float32)
        for k in range(5):
            hit = (offsets_ref[band, k] == tap).astype(jnp.float32)
            total = total + hit * filters_ref[band, k].astype(jnp.float32)
        block = total.astype(jnp.bfloat16)
        for m in range(2):
            at = tap + 3 + m
            taps[at * 128 : (at + 1) * 128, m * 128 : (m + 1) * 128] = block
    chosen = lax.broadcasted_iota(jnp.int32, (levels, 8, levels), 1) == band
    picked = jnp.sum(jnp.where(chosen, vertical_ref[...].astype(jnp.float32), 0.0), axis=1)
    vert[...] = jnp.zeros_like(vert)
    vert[0:levels, 0:levels] = picked.astype(jnp.bfloat16)

    tables = [
        pltpu.make_async_copy(taps, taps_hbm, table_sems.at[0]),
        pltpu.make_async_copy(vert, vert_hbm, table_sems.at[1]),
    ]
    for table in tables:
        table.start()

    sends = []

    def block_of(dx, dz, j):
        return ((xh + dx) % 2) * 8 + ((z + dz + 8 - y - 2 * j) % 4) * 2 + j

    def rows_of(dx, dz, n):
        return pl.ds(block_of(dx, dz, n // SPLIT) * 4 + (n % SPLIT) * nq, nq)

    def piece(dx, dz, n):
        return rows_ref.at[pl.ds(1, 2), rows_of(dx, dz, n)]

    def send(dx, dz, n, to, there, only=None):
        ref = piece(dx, dz, n)
        copy = pltpu.make_async_remote_copy(
            ref, ref, send_sems.at[len(sends)], recv_sems.at[there[0], there[1], n],
            device_id={"lon": o, "lat": to}, device_id_type=MESH,
        )
        sends.append((copy, only))
        if only is None:
            copy.start()
        else:
            pl.when(only)(copy.start)

    def halo(dx, dz, n, side, partner=False):
        q = rows_of(dx, dz, n)
        src = rows_ref.at[1 + side, q]
        dst = rows_ref.at[3 - 3 * side, q]
        slot = block_of(dx, dz, n // SPLIT) * SPLIT + n % SPLIT
        own = block_of(dx + 1, dz, n // SPLIT) * SPLIT + n % SPLIT if partner else slot
        return pltpu.make_async_remote_copy(
            src, dst, halo_send.at[side, own], halo_recv.at[side, slot],
            device_id={"lon": o - 1 + 2 * side, "lat": xp if partner else t}, device_id_type=MESH,
        )

    def start_halo(dx, dz, n, side):
        if dx == 0:
            halo(dx, dz, n, side).start()

            @pl.when(crosses(side))
            def _():
                halo(dx, dz, n, side, True).start()
        else:
            @pl.when(jnp.logical_not(crosses(side)))
            def _():
                halo(dx, dz, n, side).start()

    boundary = ((xl == 0) & (y == 3)) | ((xl == 1) & (y == 0))

    def ring_start(dx, n, only=None):
        send(dx, 0, n, zp, (dx, 3), only)
        send(dx, 0, n, zm, (dx, 1), only)

    def arrive(dx, dz, n):
        if (dx, dz) != (0, 0):
            ref = piece(dx, dz, n)
            pltpu.make_async_copy(ref, ref, recv_sems.at[dx, dz, n]).wait()
        late = n in LATE
        only = boundary if dx == 1 and late else None
        if (dx, dz) == (0, 0):
            send(dx, dz, n, xp, (1, 0))
        elif dz == 0:
            ring_start(dx, n, only)
        if dz == 3 and n < per // 2:
            send(dx, dz, n, zp, (dx, 2), only)
        if dz == 1 and n >= per // 2:
            send(dx, dz, n, zm, (dx, 2), only)
        if dx == 0 and dz != 0 and late:
            send(dx, dz, n, xp, (1, dz), jnp.logical_not(boundary))
        each_side(lambda side: start_halo(dx, dz, n, side))

    def blend_block(block):
        for s in range(SPLIT):
            for side, present in ((1, o > 0), (0, o < 15)):

                @pl.when(present)
                def _():
                    dst = rows_ref.at[3 - 3 * side, pl.ds(block * 4 + s * nq, nq)]
                    pltpu.make_async_copy(dst, dst, halo_recv.at[side, block * SPLIT + s]).wait()

        for q in range(4):
            rows = [rows_ref[i, block * 4 + q].astype(jnp.float32) for i in range(4)]
            m = (2 * block + (q + 1) // 2) % 32
            for i in range(2):
                value = w0 * rows[i] + w1 * rows[i + 1] + w2 * rows[i + 2]
                blended[i, m, 1 - q % 2] = value.astype(jnp.bfloat16)

    def keep(n, count, first):
        part = pl.ds(0, 2), pl.ds(first, count)
        return pltpu.make_async_copy(blended.at[part], blended_hbm.at[part], out_sems.at[n])

    def blend_own(n, carry):
        block = xh * 8 + n
        blend_block(block)

        @pl.when(n == 0)
        def _():
            keep(n, 1, 2 * block + 1).start()

        @pl.when(n > 0)
        def _():
            keep(n, 2, 2 * block).start()

        return carry

    def blend_other(n, carry):
        block = (1 - xh) * 8 + n
        blend_block(block)
        keep(8 + n, 2, 2 * block).start()
        return carry

    def inner_outputs():
        def body(n, carry):
            chunk_output(4 * xh + 1 + n, n, taps, vert, mixed, lambda i, m: load_pair(i, m % 32), done)
            pltpu.make_async_copy(done.at[n], inner_hbm.at[n], store_sems.at[n]).start()
            return carry

        lax.fori_loop(0, 2, body, 0)

    def load_pair(i, m):
        return jnp.concatenate([blended[i, m, 0], blended[i, m, 1]], axis=1)

    pl.semaphore_wait(shifted_sem, 3)
    for n in sorted(range(per), key=lambda n: n % SPLIT):
        ref = piece(0, 0, n)
        pltpu.make_async_copy(ref, ref, recv_sems.at[0, 0, n]).wait()
        ring_start(0, n)
    for lon, lat in peers:
        pl.semaphore_signal(ready_sem, inc=1, device_id={"lon": lon, "lat": lat}, device_id_type=MESH)
    pl.semaphore_wait(ready_sem, NPEERS)

    everything = sorted(range(per), key=lambda n: n % SPLIT)
    late = [n for n in everything if n in LATE]
    early = [n for n in everything if n not in late]
    for dx, dz, which in ORDER_1:
        for n in {"all": everything, "late": late, "early": early}[which]:
            arrive(dx, dz, n)
    lax.fori_loop(0, 8, blend_own, 0)
    inner_outputs()
    for dx, dz, which in ORDER_2:
        for n in {"all": everything, "late": late, "early": early}[which]:
            arrive(dx, dz, n)
    lax.fori_loop(0, 8, blend_other, 0)
    keep(16, 1, 16 * xh).start()

    for table in tables:
        table.wait()
    for n in range(2):
        pltpu.make_async_copy(done.at[n], inner_hbm.at[n], store_sems.at[n]).wait()
    for n in range(17):
        keep(n, 1 if n in (0, 16) else 2, 0).wait()
    for k, s in parts:
        shift(k, s, "wait")
        first(k, s, "wait")
    for copy, only in sends:
        if only is None:
            copy.wait_send()
        else:
            pl.when(only)(copy.wait_send)
    for dx in range(2):
        for dz in range(4):
            for n in range(per):
                each_side(lambda side: halo(dx, dz, n, side).wait_send())


ORDER_1 = [(0, 0, "all"), (0, 1, "all"), (0, 3, "all"), (1, 0, "all"), (0, 2, "all"), (1, 1, "all"), (1, 3, "all")]
ORDER_2 = [(1, 2, "all")]


def fused(weights, offsets, slots, x, filters, vertical, levels, pad):
    per = 2 * SPLIT
    smem, anywhere = pl.BlockSpec(memory_space=pltpu.SMEM), pl.BlockSpec(memory_space=pl.ANY)
    return pl.pallas_call(
        functools.partial(fused_kernel, levels, pad),
        out_shape=[
            jax.ShapeDtypeStruct((2, 32, 2, pad, 128), jnp.bfloat16),
            jax.ShapeDtypeStruct((2, 2, levels, 8, 128), jnp.bfloat16),
            jax.ShapeDtypeStruct((1024, 256), jnp.bfloat16),
            jax.ShapeDtypeStruct((pad, pad), jnp.bfloat16),
        ],
        in_specs=[smem, smem, smem, anywhere, anywhere, anywhere],
        out_specs=[anywhere] * 4,
        scratch_shapes=[
            pltpu.VMEM((16 * levels, 128), jnp.float32),
            pltpu.VMEM((8, 5, 128, 128), jnp.bfloat16),
            pltpu.VMEM((levels, 8, levels), jnp.bfloat16),
            pltpu.VMEM((4, 4, pad, 128), jnp.bfloat16),
            pltpu.VMEM((4, 4, pad, 128), jnp.bfloat16),
            pltpu.VMEM((4, 64, pad, 128), jnp.bfloat16),
            pltpu.VMEM((2, 32, 2, pad, 128), jnp.bfloat16),
            pltpu.VMEM((1024, 256), jnp.bfloat16),
            pltpu.VMEM((pad, pad), jnp.bfloat16),
            pltpu.VMEM((2, pad * 8, 128), jnp.float32),
            pltpu.VMEM((2, 2, levels, 8, 128), jnp.bfloat16),
            pltpu.SemaphoreType.DMA((4,)),
            pltpu.SemaphoreType.DMA((48 * SPLIT,)),
            pltpu.SemaphoreType.DMA((2, 2, SPLIT)),
            pltpu.SemaphoreType.DMA((2, SPLIT)),
            pltpu.SemaphoreType.DMA((2, 4, per)),
            pltpu.SemaphoreType.DMA((2, 8 * per)),
            pltpu.SemaphoreType.DMA((2, 8 * per)),
            pltpu.SemaphoreType.REGULAR,
            pltpu.SemaphoreType.REGULAR,
            pltpu.SemaphoreType.DMA((2,)),
            pltpu.SemaphoreType.DMA((17,)),
            pltpu.SemaphoreType.DMA((2,)),
        ],
        compiler_params=pltpu.CompilerParams(
            collective_id=0, has_side_effects=True, vmem_limit_bytes=VMEM_MIB << 20
        ),
        name="fused",
    )(weights, offsets, slots, x, filters, vertical)


NPEERS = 6
VMEM_MIB = 60
OUTER_MIB = 60


def on_device(grad_field, lat_weights, block_offsets, filters, vertical, slot_of_band):
    levels = grad_field.shape[2]
    pad = (levels + 15) // 16 * 16
    x = grad_field.transpose(0, 2, 1, 3).reshape(-1, 128)
    blended, inner, taps, vert = fused(
        lat_weights.T, block_offsets, slot_of_band, x, filters, vertical.transpose(1, 0, 2), levels, pad
    )
    out = outer_outputs(blended, inner, taps, vert, levels, pad)
    return out.transpose(0, 1, 3, 2, 4)


def solution(mesh):
    placed = (P("lat", "lon", None, None), P(), P(), P(), P(), P())
    return jax.shard_map(
        on_device,
        mesh=mesh,
        in_specs=placed,
        out_specs=P("lat", "lon", None, None, None),
        check_vma=False,
    )
```

```python
import functools

import jax
import jax.numpy as jnp
from jax import lax
from jax.experimental import pallas as pl
from jax.experimental.pallas import tpu as pltpu
from jax.sharding import PartitionSpec as P

MESH = pl.DeviceIdType.MESH
SPLIT = 2
LATE = (3,)


def chunk_output(chunk, slot, taps, vert, mixed, load_pair, done):
    levels, pad = done.shape[-3], vert.shape[0]
    lhs = []
    for i in range(2):
        pairs = [load_pair(i, chunk * 4 + n + 31) for n in range(7)]
        lhs.append(jnp.concatenate([jnp.concatenate(pairs[k : k + 4], axis=0) for k in range(4)], axis=1))
    lhs = jnp.concatenate(lhs, axis=0)
    smooth = jnp.dot(lhs, taps[...], preferred_element_type=jnp.float32).astype(jnp.bfloat16)
    wide = jnp.concatenate([smooth[p * pad : (p + 1) * pad] for p in range(8)], axis=1)
    result = jnp.dot(vert[...], wide, preferred_element_type=jnp.float32)
    for i in range(2):
        for n in range(8):
            at = (8 * i + n) * 128
            mixed[i, pl.ds(n, pad, stride=8), :] = result[:, at : at + 128]
        flat = mixed[i, 0 : levels * 8, :].reshape(levels, 8, 128)
        done[slot, i] = flat.astype(jnp.bfloat16)


def outer_kernel(levels, blended_hbm, inner_hbm, taps_hbm, vert_hbm, out_hbm, blended, taps, vert, mixed, done, ready, load_sems, inner_sems, store_sems):
    xh = lax.axis_index("lat") // 4

    def group(k):
        part = pl.ds(0, 2), pl.ds(((4 * xh + 2 + k) % 8) * 4, 4)
        return pltpu.make_async_copy(blended_hbm.at[part], blended.at[part], load_sems.at[k])

    def place(chunk):
        return out_hbm.at[0, pl.ds(0, 2), pl.ds(0, levels), pl.ds(pl.multiple_of(chunk * 8, 8), 8)]

    def store(slot, chunk):
        return pltpu.make_async_copy(done.at[slot], place(chunk), store_sems.at[slot])

    tables = [
        pltpu.make_async_copy(taps_hbm, taps, load_sems.at[8]),
        pltpu.make_async_copy(vert_hbm, vert, load_sems.at[9]),
    ]
    loads = [pltpu.make_async_copy(inner_hbm.at[n], ready.at[n], inner_sems.at[n]) for n in range(2)]
    inner = [pltpu.make_async_copy(ready.at[n], place(4 * xh + 1 + n), inner_sems.at[2 + n]) for n in range(2)]
    for k in range(3):
        group(k).start()
    for copy in tables:
        copy.start()
    for k in range(3, 8):
        group(k).start()
    for copy in loads:
        copy.start()
    for k in range(2):
        group(k).wait()
    for copy in tables:
        copy.wait()

    def load_pair(i, m):
        return jnp.concatenate([blended[i, m % 32, 0], blended[i, m % 32, 1]], axis=1)

    def body(n, carry):
        group(n + 2).wait()
        chunk = (4 * xh + 3 + n) % 8

        @pl.when(n >= 2)
        def _():
            store(n % 2, chunk).wait()

        chunk_output(chunk, n % 2, taps, vert, mixed, load_pair, done)
        store(n % 2, chunk).start()

        @pl.when(n == 2)
        def _():
            for load, copy in zip(loads, inner):
                load.wait()
                copy.start()

        return carry

    lax.fori_loop(0, 6, body, 0)
    for slot in range(2):
        store(slot, 0).wait()
    for copy in inner:
        copy.wait()


def outer_outputs(blended, inner, taps, vert, levels, pad):
    anywhere = pl.BlockSpec(memory_space=pl.ANY)
    return pl.pallas_call(
        functools.partial(outer_kernel, levels),
        out_shape=jax.ShapeDtypeStruct((1, 2, levels, 64, 128), jnp.bfloat16),
        in_specs=[anywhere] * 4,
        out_specs=anywhere,
        scratch_shapes=[
            pltpu.VMEM((2, 32, 2, pad, 128), jnp.bfloat16),
            pltpu.VMEM((1024, 256), jnp.bfloat16),
            pltpu.VMEM((pad, pad), jnp.bfloat16),
            pltpu.VMEM((2, pad * 8 + 8, 128), jnp.float32),
            pltpu.VMEM((2, 2, levels, 8, 128), jnp.bfloat16),
            pltpu.VMEM((2, 2, levels, 8, 128), jnp.bfloat16),
            pltpu.SemaphoreType.DMA((10,)),
            pltpu.SemaphoreType.DMA((4,)),
            pltpu.SemaphoreType.DMA((2,)),
        ],
        compiler_params=pltpu.CompilerParams(vmem_limit_bytes=OUTER_MIB << 20),
        name="outer_outputs",
    )(blended, inner, taps, vert)


def fused_kernel(
    levels, pad,
    weights_ref, offsets_ref, slots_ref, x_hbm, filters_hbm, vertical_hbm,
    blended_hbm, inner_hbm, taps_hbm, vert_hbm,
    x_ref, filters_ref, vertical_ref, staged, shifted, rows_ref, blended, taps, vert, mixed, done,
    load_sems, send_sems, shift_sems, first_sems, recv_sems, halo_send, halo_recv, ready_sem, shifted_sem, store_sems, out_sems, table_sems,
):
    o, t = lax.axis_index("lon"), lax.axis_index("lat")
    xh, z = t // 4, t % 4
    xl, y, core = o // 8, (o // 2) % 4, o % 2
    x = 2 * xh + xl
    zp, zm = xh * 4 + (z + 1) % 4, xh * 4 + (z + 3) % 4
    xp = (1 - xh) * 4 + z
    nq = 4 // SPLIT
    per = 2 * SPLIT
    half = 2 * levels * 4

    x_loads = [
        pltpu.make_async_copy(x_hbm.at[pl.ds(k * half, half)], x_ref.at[pl.ds(k * half, half)], load_sems.at[k])
        for k in range(2)
    ]
    weight_loads = [
        pltpu.make_async_copy(filters_hbm, filters_ref, load_sems.at[2]),
        pltpu.make_async_copy(vertical_hbm, vertical_ref, load_sems.at[3]),
    ]
    for load in x_loads:
        load.start()

    ahead = (y + 2 * core) % 4
    row_group = (z + 8 - y - 2 * core) % 4
    swapped = xh * 8 + y * 2 + core

    def shift_to(k):
        return (swapped, xl * 4 + (z + ahead) % 4) if k == 0 else (o, xh * 4 + (z + ahead) % 4)

    def shift_from(k):
        return (swapped, xl * 4 + (z + 4 - ahead) % 4) if k == 0 else (o, xh * 4 + (z + 4 - ahead) % 4)

    def stays(k):
        return (ahead == 0) & (xh == xl) if k == 0 else ahead == 0

    def relay(k):
        return (xl * 8 + row_group * 2, t) if k == 0 else (xh * 8 + row_group * 2 + 1, xl * 4 + z)

    def source(j):
        place = ((z + 8 - y - 2 * j) % 4) * 2 + j
        return jnp.where(core == 0, xl, xh) * 8 + place, jnp.where(core == 0, t, xl * 4 + z)

    barrier = pltpu.get_barrier_semaphore()

    def greet(lon, lat):
        pl.semaphore_signal(barrier, inc=1, device_id={"lon": lon, "lat": lat}, device_id_type=MESH)

    for k in range(2):
        greet(*shift_to(k))
        greet(*shift_from(k))
        greet(*relay(k))
        greet(*source(k))
    for lat in (zp, zm, xp):
        greet(o, lat)
    peers = [(o, xh * 4 + (z + n) % 4) for n in (1, 2, 3)]
    peers += [(((x + n) % 2) * 8 + y * 2 + core, ((x + n) % 4) // 2 * 4 + z) for n in (1, 2, 3)]
    for lon, lat in peers:
        greet(lon, lat)

    def each_side(action):
        @pl.when(o > 0)
        def _():
            action(0)

        @pl.when(o < 15)
        def _():
            action(1)

    def crosses(side):
        return o == (8 if side == 0 else 7)

    def greet_side(side):
        greet(o - 1 + 2 * side, t)
        greet(o - 1 + 2 * side, jnp.where(crosses(side), xp, t))

    each_side(greet_side)

    def stage(k):
        for i in (2 * k, 2 * k + 1):
            for q in range(4):
                value = x_ref[pl.ds(i * levels * 4 + q, levels, stride=4), :]
                staged[i, q, 0:levels, :] = value.astype(jnp.bfloat16)
                staged[i, q, levels:pad, :] = jnp.zeros((pad - levels, 128), jnp.bfloat16)

    def shift(k, s, action):
        at = (pl.ds(2 * k, 2), pl.ds(s * nq, nq))
        src, dst = staged.at[at], shifted.at[at]

        @pl.when(stays(k))
        def _():
            if action == "start":
                pltpu.make_async_copy(src, dst, shift_sems.at[1, k, s]).start()

        @pl.when(jnp.logical_not(stays(k)))
        def _():
            far = pltpu.make_async_remote_copy(
                src, dst, shift_sems.at[0, k, s], shift_sems.at[1, k, s],
                device_id={"lon": shift_to(k)[0], "lat": shift_to(k)[1]}, device_id_type=MESH,
            )
            if action == "start":
                far.start()
            else:
                far.wait_send()

    def first(k, s, action):
        src = shifted.at[pl.ds(2 * k, 2), pl.ds(s * nq, nq)]
        dst = rows_ref.at[pl.ds(1, 2), pl.ds(4 * (swapped if k == 0 else o) + s * nq, nq)]
        here = recv_sems.at[0, 0, core * SPLIT + s]
        lon, lat = relay(k)
        mine = (lat == t) & (lon == o)

        @pl.when(mine)
        def _():
            if action == "start":
                pltpu.make_async_copy(src, dst, here).start()

        @pl.when(jnp.logical_not(mine))
        def _():
            far = pltpu.make_async_remote_copy(
                src, dst, first_sems.at[k, s], here,
                device_id={"lon": lon, "lat": lat}, device_id_type=MESH,
            )
            if action == "start":
                far.start()
            else:
                far.wait_send()

    edge = (o == 0).astype(jnp.int32) + (o == 15).astype(jnp.int32)
    x_loads[0].wait()
    stage(0)
    pl.semaphore_wait(barrier, 21 - 2 * edge)
    parts = [(k, s) for s in range(SPLIT) for k in range(2)]
    for s in range(SPLIT):
        shift(0, s, "start")
    x_loads[1].wait()
    stage(1)
    for s in range(SPLIT):
        shift(1, s, "start")
    for load in weight_loads:
        load.start()

    for k, s in parts:
        dst = shifted.at[pl.ds(2 * k, 2), pl.ds(s * nq, nq)]
        pltpu.make_async_copy(dst, dst, shift_sems.at[1, k, s]).wait()
        first(k, s, "start")

    for lon, lat in peers[:3]:
        pl.semaphore_signal(shifted_sem, inc=1, device_id={"lon": lon, "lat": lat}, device_id_type=MESH)

    @pl.when(edge > 0)
    def _():
        row = jnp.where(o == 0, 0, 3)

        def fill(q, carry):
            rows_ref[row, q] = jnp.zeros((pad, 128), jnp.bfloat16)
            return carry

        lax.fori_loop(0, 64, fill, 0)

    band = jnp.int32(0)
    for b in range(8):
        band = jnp.where(slots_ref[b] == t, b, band)
    w0, w1, w2 = weights_ref[0, band], weights_ref[1, band], weights_ref[2, band]
    for load in weight_loads:
        load.wait()
    taps[...] = jnp.zeros_like(taps)
    for tap in range(-3, 4):
        total = jnp.zeros((128, 128), jnp.float32)
        for k in range(5):
            hit = (offsets_ref[band, k] == tap).astype(jnp.float32)
            total = total + hit * filters_ref[band, k].astype(jnp.float32)
        block = total.astype(jnp.bfloat16)
        for m in range(2):
            at = tap + 3 + m
            taps[at * 128 : (at + 1) * 128, m * 128 : (m + 1) * 128] = block
    chosen = lax.broadcasted_iota(jnp.int32, (levels, 8, levels), 1) == band
    picked = jnp.sum(jnp.where(chosen, vertical_ref[...].astype(jnp.float32), 0.0), axis=1)
    vert[...] = jnp.zeros_like(vert)
    vert[0:levels, 0:levels] = picked.astype(jnp.bfloat16)

    tables = [
        pltpu.make_async_copy(taps, taps_hbm, table_sems.at[0]),
        pltpu.make_async_copy(vert, vert_hbm, table_sems.at[1]),
    ]
    for table in tables:
        table.start()

    sends = []

    def block_of(dx, dz, j):
        return ((xh + dx) % 2) * 8 + ((z + dz + 8 - y - 2 * j) % 4) * 2 + j

    def rows_of(dx, dz, n):
        return pl.ds(block_of(dx, dz, n // SPLIT) * 4 + (n % SPLIT) * nq, nq)

    def piece(dx, dz, n):
        return rows_ref.at[pl.ds(1, 2), rows_of(dx, dz, n)]

    def send(dx, dz, n, to, there, only=None):
        ref = piece(dx, dz, n)
        copy = pltpu.make_async_remote_copy(
            ref, ref, send_sems.at[len(sends)], recv_sems.at[there[0], there[1], n],
            device_id={"lon": o, "lat": to}, device_id_type=MESH,
        )
        sends.append((copy, only))
        if only is None:
            copy.start()
        else:
            pl.when(only)(copy.start)

    def halo(dx, dz, n, side, partner=False):
        q = rows_of(dx, dz, n)
        src = rows_ref.at[1 + side, q]
        dst = rows_ref.at[3 - 3 * side, q]
        slot = block_of(dx, dz, n // SPLIT) * SPLIT + n % SPLIT
        own = block_of(dx + 1, dz, n // SPLIT) * SPLIT + n % SPLIT if partner else slot
        return pltpu.make_async_remote_copy(
            src, dst, halo_send.at[side, own], halo_recv.at[side, slot],
            device_id={"lon": o - 1 + 2 * side, "lat": xp if partner else t}, device_id_type=MESH,
        )

    def start_halo(dx, dz, n, side):
        if dx == 0:
            halo(dx, dz, n, side).start()

            @pl.when(crosses(side))
            def _():
                halo(dx, dz, n, side, True).start()
        else:
            @pl.when(jnp.logical_not(crosses(side)))
            def _():
                halo(dx, dz, n, side).start()

    boundary = ((xl == 0) & (y == 3)) | ((xl == 1) & (y == 0))

    def ring_start(dx, n, only=None):
        send(dx, 0, n, zp, (dx, 3), only)
        send(dx, 0, n, zm, (dx, 1), only)

    def arrive(dx, dz, n):
        if (dx, dz) != (0, 0):
            ref = piece(dx, dz, n)
            pltpu.make_async_copy(ref, ref, recv_sems.at[dx, dz, n]).wait()
        late = n in LATE
        only = boundary if dx == 1 and late else None
        if (dx, dz) == (0, 0):
            send(dx, dz, n, xp, (1, 0))
        elif dz == 0:
            ring_start(dx, n, only)
        if dz == 3 and n < per // 2:
            send(dx, dz, n, zp, (dx, 2), only)
        if dz == 1 and n >= per // 2:
            send(dx, dz, n, zm, (dx, 2), only)
        if dx == 0 and dz != 0 and late:
            send(dx, dz, n, xp, (1, dz), jnp.logical_not(boundary))
        each_side(lambda side: start_halo(dx, dz, n, side))

    def blend_block(block):
        for s in range(SPLIT):
            for side, present in ((1, o > 0), (0, o < 15)):

                @pl.when(present)
                def _():
                    dst = rows_ref.at[3 - 3 * side, pl.ds(block * 4 + s * nq, nq)]
                    pltpu.make_async_copy(dst, dst, halo_recv.at[side, block * SPLIT + s]).wait()

        for q in range(4):
            rows = [rows_ref[i, block * 4 + q].astype(jnp.float32) for i in range(4)]
            m = (2 * block + (q + 1) // 2) % 32
            for i in range(2):
                value = w0 * rows[i] + w1 * rows[i + 1] + w2 * rows[i + 2]
                blended[i, m, 1 - q % 2] = value.astype(jnp.bfloat16)

    def keep(n, count, first):
        part = pl.ds(0, 2), pl.ds(first, count)
        return pltpu.make_async_copy(blended.at[part], blended_hbm.at[part], out_sems.at[n])

    def blend_own(n, carry):
        block = xh * 8 + n
        blend_block(block)

        @pl.when(n == 0)
        def _():
            keep(n, 1, 2 * block + 1).start()

        @pl.when(n > 0)
        def _():
            keep(n, 2, 2 * block).start()

        return carry

    def blend_other(n, carry):
        block = (1 - xh) * 8 + n
        blend_block(block)
        keep(8 + n, 2, 2 * block).start()
        return carry

    def inner_outputs():
        def body(n, carry):
            chunk_output(4 * xh + 1 + n, n, taps, vert, mixed, lambda i, m: load_pair(i, m % 32), done)
            pltpu.make_async_copy(done.at[n], inner_hbm.at[n], store_sems.at[n]).start()
            return carry

        lax.fori_loop(0, 2, body, 0)

    def load_pair(i, m):
        return jnp.concatenate([blended[i, m, 0], blended[i, m, 1]], axis=1)

    pl.semaphore_wait(shifted_sem, 3)
    for n in sorted(range(per), key=lambda n: n % SPLIT):
        ref = piece(0, 0, n)
        pltpu.make_async_copy(ref, ref, recv_sems.at[0, 0, n]).wait()
        ring_start(0, n)
    for lon, lat in peers:
        pl.semaphore_signal(ready_sem, inc=1, device_id={"lon": lon, "lat": lat}, device_id_type=MESH)
    pl.semaphore_wait(ready_sem, NPEERS)

    everything = sorted(range(per), key=lambda n: n % SPLIT)
    late = [n for n in everything if n in LATE]
    early = [n for n in everything if n not in late]
    for dx, dz, which in ORDER_1:
        for n in {"all": everything, "late": late, "early": early}[which]:
            arrive(dx, dz, n)
    lax.fori_loop(0, 8, blend_own, 0)
    inner_outputs()
    for dx, dz, which in ORDER_2:
        for n in {"all": everything, "late": late, "early": early}[which]:
            arrive(dx, dz, n)
    lax.fori_loop(0, 8, blend_other, 0)
    keep(16, 1, 16 * xh).start()

    for table in tables:
        table.wait()
    for n in range(2):
        pltpu.make_async_copy(done.at[n], inner_hbm.at[n], store_sems.at[n]).wait()
    for n in range(17):
        keep(n, 1 if n in (0, 16) else 2, 0).wait()
    for k, s in parts:
        shift(k, s, "wait")
        first(k, s, "wait")
    for copy, only in sends:
        if only is None:
            copy.wait_send()
        else:
            pl.when(only)(copy.wait_send)
    for dx in range(2):
        for dz in range(4):
            for n in range(per):
                each_side(lambda side: halo(dx, dz, n, side).wait_send())


ORDER_1 = [(0, 0, "all"), (0, 1, "all"), (0, 3, "all"), (1, 0, "all"), (0, 2, "all"), (1, 1, "all"), (1, 3, "all")]
ORDER_2 = [(1, 2, "all")]


def fused(weights, offsets, slots, x, filters, vertical, levels, pad):
    per = 2 * SPLIT
    smem, anywhere = pl.BlockSpec(memory_space=pltpu.SMEM), pl.BlockSpec(memory_space=pl.ANY)
    return pl.pallas_call(
        functools.partial(fused_kernel, levels, pad),
        out_shape=[
            jax.ShapeDtypeStruct((2, 32, 2, pad, 128), jnp.bfloat16),
            jax.ShapeDtypeStruct((2, 2, levels, 8, 128), jnp.bfloat16),
            jax.ShapeDtypeStruct((1024, 256), jnp.bfloat16),
            jax.ShapeDtypeStruct((pad, pad), jnp.bfloat16),
        ],
        in_specs=[smem, smem, smem, anywhere, anywhere, anywhere],
        out_specs=[anywhere] * 4,
        scratch_shapes=[
            pltpu.VMEM((16 * levels + 8, 128), jnp.float32),
            pltpu.VMEM((8, 5, 128, 128), jnp.bfloat16),
            pltpu.VMEM((levels, 8, levels), jnp.bfloat16),
            pltpu.VMEM((4, 4, pad, 128), jnp.bfloat16),
            pltpu.VMEM((4, 4, pad, 128), jnp.bfloat16),
            pltpu.VMEM((4, 64, pad, 128), jnp.bfloat16),
            pltpu.VMEM((2, 32, 2, pad, 128), jnp.bfloat16),
            pltpu.VMEM((1024, 256), jnp.bfloat16),
            pltpu.VMEM((pad, pad), jnp.bfloat16),
            pltpu.VMEM((2, pad * 8 + 8, 128), jnp.float32),
            pltpu.VMEM((2, 2, levels, 8, 128), jnp.bfloat16),
            pltpu.SemaphoreType.DMA((4,)),
            pltpu.SemaphoreType.DMA((48 * SPLIT,)),
            pltpu.SemaphoreType.DMA((2, 2, SPLIT)),
            pltpu.SemaphoreType.DMA((2, SPLIT)),
            pltpu.SemaphoreType.DMA((2, 4, per)),
            pltpu.SemaphoreType.DMA((2, 8 * per)),
            pltpu.SemaphoreType.DMA((2, 8 * per)),
            pltpu.SemaphoreType.REGULAR,
            pltpu.SemaphoreType.REGULAR,
            pltpu.SemaphoreType.DMA((2,)),
            pltpu.SemaphoreType.DMA((17,)),
            pltpu.SemaphoreType.DMA((2,)),
        ],
        compiler_params=pltpu.CompilerParams(
            collective_id=0, has_side_effects=True, vmem_limit_bytes=VMEM_MIB << 20
        ),
        name="fused",
    )(weights, offsets, slots, x, filters, vertical)


NPEERS = 6
VMEM_MIB = 60
OUTER_MIB = 60


def on_device(grad_field, lat_weights, block_offsets, filters, vertical, slot_of_band):
    levels = grad_field.shape[2]
    pad = (levels + 15) // 16 * 16
    x = grad_field.transpose(0, 2, 1, 3).reshape(-1, 128)
    blended, inner, taps, vert = fused(
        lat_weights.T, block_offsets, slot_of_band, x, filters, vertical.transpose(1, 0, 2), levels, pad
    )
    out = outer_outputs(blended, inner, taps, vert, levels, pad)
    return out.transpose(0, 1, 3, 2, 4)


def solution(mesh):
    placed = (P("lat", "lon", None, None), P(), P(), P(), P(), P())
    return jax.shard_map(
        on_device,
        mesh=mesh,
        in_specs=placed,
        out_specs=P("lat", "lon", None, None, None),
        check_vma=False,
    )
```
